32 devices in a mesh: depth: 4 (over z), rows: 8 (over y, x, core).
Axes of the slice: x: 2, y: 2, z: 4, core: 2. Of those that a mesh axis runs over, the one named last changes fastest.
Arguments:
- density: float32 [64, 1024, 2048], P('depth', 'rows'), may hold values from 0.2 to 3
- occupancy: int32 [4, 8, 16], P('depth', 'rows'), may hold values from 0 to 1, as said below
- transfer: float32 [2, 4], replicated, may hold values from -1.5 to 1.5
Outputs:
- image: float32 [4, 1024, 2048], P(None, 'rows', 'depth')
The draws below stay inside these ranges and needn't reach their ends.
Inputs may be any that keep to these rules, and one draw needn't show every extreme that they name: `occupancy`: each entry is 0 or 1 and flags a block of 16 x 128 x 128 cells as occupied; at most 12 of the blocks of one device's brick are occupied, and some brick has exactly 12.
All inputs are finite; a program needn't handle non-finite values.
Results may differ from the reference program's by a relative error of at most 0.000079.
Values sent between devices are 32-bit elements; how exact they have to be, the bound alone decides.
No kernel may reach another device: no remote copies, remote signals or barrier semaphores. Data moves between devices by JAX's collectives and lax.ppermute only.
A program may use at most 256 MiB of HBM per device.

```python
import math
import jax
import jax.numpy as jnp
from jax import lax

BZ = 16
BY = 128
NX = 2048
CB = 128
OCCMAX = 12
NZ = 64
NY = 1024


def draw_occupancy(key, part):
    brick_count = NZ // BZ * (NY // BY)
    block_count = NX // CB
    first_key, second_key, third_key = jax.random.split(key, 3)
    counts = jax.random.randint(first_key, (brick_count,), max(OCCMAX // 3, 1), OCCMAX + 1)
    full_brick = jax.random.randint(second_key, (), 0, brick_count)
    counts = jnp.where(jnp.arange(brick_count) == full_brick, OCCMAX, counts)
    scores = jax.random.randint(third_key, (brick_count, block_count), 0, 1 << 20) * block_count + jnp.arange(block_count)
    ranks = jnp.argsort(jnp.argsort(scores, axis=1), axis=1)
    flags = (ranks < counts[:, None]).astype(jnp.int32)
    return flags.reshape(NZ // BZ, NY // BY, block_count)


def block_levels(stream_key, dims, cuts, smallest, high):
    level, own = 1.0, jax.random.fold_in(stream_key, 6)
    for axis_at, shards_of in cuts:
        draws = jnp.exp(jax.random.uniform(jax.random.fold_in(own, axis_at), (shards_of,), jnp.float32, smallest / len(cuts), high / len(cuts)))
        level = level * jnp.repeat(draws, dims[axis_at] // shards_of).reshape([-1 if axis == axis_at else 1 for axis in range(len(dims))])
    return level


def setup_inputs(seed: int = 0) -> dict:
    key_of = jax.random.split(jax.random.key(seed), 4)
    density = jnp.clip(jnp.exp(math.log(3.0) - 2.7080502 * jax.random.uniform(key_of[0], (NZ, NY, NX), jnp.float32) ** block_levels(key_of[0], (NZ, NY, NX), ((0, 4), (1, 8)), -0.2, 0.2)), 0.2, 3.0)
    occupancy = draw_occupancy(jax.random.fold_in(key_of[3], 71), 0)
    transfer = jnp.clip(jax.random.uniform(key_of[2], (2, 4), jnp.float32, -1.5, 1.5), -1.5, 1.5)
    return dict(density=density, occupancy=occupancy, transfer=transfer)


def voxels(window, transfer, ray_step):
    center = window[1, 1:-1, ..., 1:-1]
    grad_z = (window[2, 1:-1, ..., 1:-1] - window[0, 1:-1, ..., 1:-1]) * 0.5
    grad_y = (window[1, 2:, ..., 1:-1] - window[1, :-2, ..., 1:-1]) * 0.5
    grad_x = (window[1, 1:-1, ..., 2:] - window[1, 1:-1, ..., :-2]) * 0.5
    inv_norm = 1.0 / jnp.sqrt(grad_x * grad_x + grad_y * grad_y + grad_z * grad_z + 1.0)
    lighting = 0.3 + 0.7 * jnp.abs((0.48 * grad_z + 0.6 * grad_y + 0.64 * grad_x) * inv_norm)
    extinct = center * jax.nn.softplus(transfer[0, 3] * center + transfer[1, 3])
    opacity = 1.0 - jnp.exp(-ray_step * extinct)
    colors = jnp.stack([jax.nn.sigmoid(transfer[0, channel] * center + transfer[1, channel]) for channel in range(3)])
    return (opacity * lighting * colors, opacity)

def march(padded, transfer, ray_step):
    depth_count = padded.shape[0] - 2
    cell_shape = (padded.shape[1] - 2,) + padded.shape[2:-1] + (padded.shape[-1] - 2,)
    start_state = (jnp.zeros((3,) + cell_shape, jnp.float32), jnp.ones(cell_shape, jnp.float32))

    def advance(state_pair, depth_at):
        color_sum, transmit = state_pair
        window = lax.dynamic_slice_in_dim(padded, depth_at, 3, 0)
        shaded, opacity = voxels(window, transfer, ray_step)
        return ((color_sum + transmit * shaded, transmit * (1.0 - opacity)), None)
    (color_sum, transmit), _ = lax.scan(advance, start_state, jnp.arange(depth_count, dtype=jnp.int32))
    return (color_sum, transmit)

def reference(density, occupancy, transfer):
    block_flags = occupancy.astype(jnp.float32)
    blocks = density.reshape(NZ // BZ, BZ, NY // BY, BY, NX // CB, CB)
    masked = (blocks * block_flags[:, None, :, None, :, None]).reshape(NZ, NY, NX)
    padded = jnp.pad(masked, 1)
    ray_step = 2.0 / NZ

    def row_slab(slab_index):
        part_rows = lax.dynamic_slice_in_dim(padded, slab_index * BY, BY + 2, 1)
        color_sum, transmit = march(part_rows, transfer, ray_step)
        return jnp.concatenate([color_sum, (1.0 - transmit)[None]], 0)
    pieces = lax.map(row_slab, jnp.arange(NY // BY, dtype=jnp.int32))
    return jnp.transpose(pieces, (1, 0, 2, 3)).reshape(4, NY, NX)
```

```python
import functools
import jax
import jax.numpy as jnp
from jax import lax
from jax.experimental import pallas as pl
from jax.experimental.pallas import tpu as pltpu
from jax.sharding import PartitionSpec as P

OCCUPIED_MOST = 12
PAD = 8
ROWS_AT_ONCE = 16
LOG2_E = 1.4426950408889634
SMEM = pl.BlockSpec(memory_space=pltpu.SMEM)
VMEM = pl.BlockSpec(memory_space=pltpu.VMEM)
ANY = pl.BlockSpec(memory_space=pl.ANY)


def pack_kernel(width, flags, density, head, tail, first_row, last_row, top, bottom, plane_sem, row_sem):
    depth_cells, row_cells, _ = density.shape
    block_count = flags.shape[0]
    slots = head.shape[0] // row_cells
    top_copy = pltpu.make_async_copy(density.at[:, 0:8, :], top, row_sem.at[0])
    bottom_copy = pltpu.make_async_copy(density.at[:, row_cells - 8 : row_cells, :], bottom, row_sem.at[1])
    top_copy.start()
    bottom_copy.start()

    def copies(block, slot):
        columns = pl.ds(pl.multiple_of(block * width, width), width)
        rows = pl.ds(pl.multiple_of(slot * row_cells, row_cells), row_cells)
        return (
            pltpu.make_async_copy(density.at[0, :, columns], head.at[rows, :], plane_sem.at[0, slot]),
            pltpu.make_async_copy(density.at[depth_cells - 1, :, columns], tail.at[rows, :], plane_sem.at[1, slot]),
        )

    def begin(block, slot):
        wanted = jnp.logical_and(flags[block] > 0, slot < slots)

        @pl.when(wanted)
        def _():
            for copy in copies(block, slot):
                copy.start()

        return slot + wanted.astype(jnp.int32)

    used = lax.fori_loop(0, block_count, begin, jnp.int32(0))
    top_copy.wait()
    bottom_copy.wait()

    def edge(block, carry):
        columns = pl.ds(pl.multiple_of(block * width, width), width)
        flag = flags[block].astype(jnp.float32)
        for z in range(depth_cells):
            first_row[pl.ds(z, 1), columns] = top[z, 0:1, columns] * flag
            last_row[pl.ds(z, 1), columns] = bottom[z, 7:8, columns] * flag
        return carry

    lax.fori_loop(0, block_count, edge, 0)

    def end(slot, carry):
        for copy in copies(0, slot):
            copy.wait()
        return carry

    lax.fori_loop(0, used, end, 0)


def pack(density, flags, width):
    depth_cells, row_cells, col_cells = density.shape
    slots = min(OCCUPIED_MOST, flags.shape[0])
    plane = jax.ShapeDtypeStruct((slots * row_cells, width), jnp.float32)
    row = jax.ShapeDtypeStruct((depth_cells, col_cells), jnp.float32)
    return pl.pallas_call(
        functools.partial(pack_kernel, width),
        out_shape=(plane, plane, row, row),
        in_specs=[SMEM, ANY],
        out_specs=[VMEM] * 4,
        scratch_shapes=[
            pltpu.VMEM((depth_cells, 8, col_cells), jnp.float32),
            pltpu.VMEM((depth_cells, 8, col_cells), jnp.float32),
            pltpu.SemaphoreType.DMA((2, slots)),
            pltpu.SemaphoreType.DMA((2,)),
        ],
        name="pack",
    )(flags, density)


def shade_kernel(
    first_at,
    piece_total,
    width,
    ray_step,
    flags,
    low_flags,
    high_flags,
    turned,
    transfer,
    density,
    low_plane,
    high_plane,
    above,
    below,
    out,
    vol,
    block_sem,
    plane_sem,
):
    depth_cells, row_cells, _ = density.shape
    block_count = flags.shape[0]
    piece_blocks = block_count // piece_total
    piece_count = out.shape[0]
    own = piece_count * piece_blocks
    zero_slot = own + 2
    backward = turned[0] > 0
    first_piece = jnp.where(backward, first_at, piece_total - first_at - piece_count)
    first_block = first_piece * piece_blocks
    body = pl.ds(PAD, row_cells)

    def block_of(slot):
        return first_block + slot - 1

    def occupied(block):
        inside = jnp.logical_and(block >= 0, block < block_count)
        return jnp.logical_and(inside, flags[jnp.clip(block, 0, block_count - 1)] > 0)

    def block_copy(slot):
        block = jnp.clip(block_of(slot), 0, block_count - 1)
        columns = pl.ds(pl.multiple_of(block * width, width), width)
        return pltpu.make_async_copy(
            density.at[:, :, columns], vol.at[slot, pl.ds(1, depth_cells), body, :], block_sem.at[slot]
        )

    def low_copy(slot, rank):
        rows = pl.ds(pl.multiple_of(rank * row_cells, row_cells), row_cells)
        return pltpu.make_async_copy(low_plane.at[rows, :], vol.at[slot, 0, body, :], plane_sem.at[0, slot])

    def high_copy(slot, rank):
        rows = pl.ds(pl.multiple_of(rank * row_cells, row_cells), row_cells)
        return pltpu.make_async_copy(
            high_plane.at[rows, :], vol.at[slot, depth_cells + 1, body, :], plane_sem.at[1, slot]
        )

    def begin_block(slot, carry):
        @pl.when(occupied(block_of(slot)))
        def _():
            block_copy(slot).start()

        return carry

    lax.fori_loop(0, own + 2, begin_block, 0)

    def begin_plane(block, ranks):
        low_rank, high_rank = ranks
        slot = block - first_block + 1
        mine = jnp.logical_and(jnp.logical_and(slot >= 1, slot <= own), flags[block] > 0)
        low = low_flags[block] > 0
        high = high_flags[block] > 0

        @pl.when(jnp.logical_and(mine, low))
        def _():
            low_copy(slot, low_rank).start()

        @pl.when(jnp.logical_and(mine, high))
        def _():
            high_copy(slot, high_rank).start()

        return (low_rank + low.astype(jnp.int32), high_rank + high.astype(jnp.int32))

    lax.fori_loop(0, block_count, begin_plane, (jnp.int32(0), jnp.int32(0)))

    def clear(z, carry):
        vol[zero_slot, z, body, :] = jnp.zeros((row_cells, width), jnp.float32)
        return carry

    lax.fori_loop(1, depth_cells + 1, clear, 0)

    def arrive(slot):
        @pl.when(occupied(block_of(slot)))
        def _():
            block_copy(slot).wait()

    arrive(0)
    arrive(1)

    def visit(slot, carry):
        block = block_of(slot)
        piece = block // piece_blocks - first_piece
        place = jnp.where(backward, piece, piece_count - 1 - piece)
        columns = pl.ds(pl.multiple_of(lax.rem(block, piece_blocks) * width, width), width)
        arrive(slot + 1)

        @pl.when(jnp.logical_not(occupied(block)))
        def _():
            for channel in range(4):
                out[place, channel, :, columns] = jnp.full((row_cells, width), 1.0 if channel == 3 else 0.0, jnp.float32)

        @pl.when(occupied(block))
        def _():
            left = jnp.where(occupied(block - 1), slot - 1, zero_slot)
            right = jnp.where(occupied(block + 1), slot + 1, zero_slot)
            source = pl.ds(pl.multiple_of(block * width, width), width)
            for z in range(depth_cells):
                vol[slot, z + 1, pl.ds(PAD - 1, 1), :] = above[pl.ds(z, 1), source]
                vol[slot, z + 1, pl.ds(PAD + row_cells, 1), :] = below[pl.ds(z, 1), source]
            for side, side_flags, plane_copy in ((0, low_flags, low_copy), (1, high_flags, high_copy)):
                near = side_flags[block] > 0

                @pl.when(near)
                def _():
                    plane_copy(slot, 0).wait()

                @pl.when(jnp.logical_not(near))
                def _():
                    vol[slot, side * (depth_cells + 1), body, :] = jnp.zeros((row_cells, width), jnp.float32)

            march(slot, left, right, place, columns)

        return carry

    def march(slot, left, right, place, columns):
        rows_at_once = ROWS_AT_ONCE
        shape = (rows_at_once, width)
        lane = lax.broadcasted_iota(jnp.int32, shape, 1)
        at_first = lane == 0
        at_last = lane == width - 1
        slopes = [transfer[0, channel] * 0.5 for channel in range(3)]
        offsets = [transfer[1, channel] * 0.5 for channel in range(3)]
        decay_slope = transfer[0, 3] * LOG2_E
        decay_offset = transfer[1, 3] * LOG2_E

        def chunk(at, carry):
            start = pl.multiple_of(PAD + at * rows_at_once, 8)
            rows = pl.ds(start, rows_at_once)
            previous = vol[slot, 0, rows, :]
            center = vol[slot, 1, rows, :]
            transmit = jnp.ones(shape, jnp.float32)
            plain = jnp.zeros(shape, jnp.float32)
            tinted = [jnp.zeros(shape, jnp.float32) for _ in range(3)]
            for z in range(1, depth_cells + 1):
                following = vol[slot, z + 1, rows, :]
                diff_z = following - previous
                diff_y = vol[slot, z, pl.ds(start + 1, rows_at_once), :] - vol[slot, z, pl.ds(start - 1, rows_at_once), :]
                right_side = pltpu.roll(jnp.where(at_first, vol[right, z, rows, :], center), width - 1, 1)
                left_side = pltpu.roll(jnp.where(at_last, vol[left, z, rows, :], center), 1, 1)
                diff_x = right_side - left_side
                facing = jnp.abs(diff_x + 0.9375 * diff_y + 0.75 * diff_z)
                norm = lax.rsqrt(diff_x * diff_x + diff_y * diff_y + (diff_z * diff_z + 4.0))
                lighting = facing * norm + (0.3 / 0.448)
                soft = jnp.log(1.0 + jnp.exp2(decay_slope * center + decay_offset))
                passed = transmit * jnp.exp2((center * (-ray_step * LOG2_E)) * soft)
                weight = (transmit - passed) * lighting
                transmit = passed
                plain = plain + weight
                for channel in range(3):
                    tinted[channel] = tinted[channel] + weight * jnp.tanh(slopes[channel] * center + offsets[channel])
                previous, center = center, following
            target = pl.ds(pl.multiple_of(at * rows_at_once, 8), rows_at_once)
            for channel in range(3):
                out[place, channel, target, columns] = 0.224 * (plain + tinted[channel])
            out[place, 3, target, columns] = transmit
            return carry

        lax.fori_loop(0, row_cells // rows_at_once, chunk, 0)

    lax.fori_loop(1, own + 1, visit, 0)


def shade(first_at, piece_count, piece_total, ray_step, flags, low_flags, high_flags, turned, transfer, density, low_plane, high_plane, above, below):
    depth_cells, row_cells, col_cells = density.shape
    block_count = flags.shape[0]
    width = col_cells // block_count
    own = piece_count * (block_count // piece_total)
    cells = own * depth_cells * row_cells * width
    return pl.pallas_call(
        functools.partial(shade_kernel, first_at, piece_total, width, ray_step),
        out_shape=jax.ShapeDtypeStruct((piece_count, 4, row_cells, col_cells // piece_total), jnp.float32),
        in_specs=[SMEM] * 5 + [ANY] * 3 + [VMEM] * 2,
        out_specs=VMEM,
        scratch_shapes=[
            pltpu.VMEM((own + 3, depth_cells + 2, row_cells + 2 * PAD, width), jnp.float32),
            pltpu.SemaphoreType.DMA((own + 2,)),
            pltpu.SemaphoreType.DMA((2, own + 2)),
        ],
        compiler_params=pltpu.CompilerParams(vmem_limit_bytes=48 << 20),
        cost_estimate=pl.CostEstimate(flops=60 * cells, bytes_accessed=4 * cells, transcendentals=7 * cells),
        name=f"shade_{first_at}",
    )(flags, low_flags, high_flags, turned, transfer, density, low_plane, high_plane, above, below)


def blend_over(front_part, back_part):
    color_sum = front_part[:3] + front_part[3:] * back_part[:3]
    transmit = front_part[3:] * back_part[3:]
    return jnp.concatenate([color_sum, transmit], 0)


def clear_unless(part, present):
    return jnp.concatenate([part[:3], jnp.where(present, part[3:], 1.0)], 0)


def shards(density, occupancy, transfer):
    depth_cells, row_cells, col_cells = density.shape
    flags = occupancy.reshape(-1)
    block_count = flags.shape[0]
    width = col_cells // block_count
    count = lax.axis_size("depth")
    slabs = lax.axis_size("rows")
    position = lax.axis_index("depth")
    ray_step = 2.0 / (depth_cells * count)
    later = [(i, i + 1) for i in range(count - 1)]
    sooner = [(i + 1, i) for i in range(count - 1)]

    head, tail, first_row, last_row = pack(density, flags, width)
    low_plane = lax.ppermute(tail, "depth", later)
    high_plane = lax.ppermute(head, "depth", sooner)
    low_flags = lax.ppermute(flags, "depth", later)
    high_flags = lax.ppermute(flags, "depth", sooner)
    above = lax.ppermute(last_row, "rows", [(i, i + 1) for i in range(slabs - 1)])
    below = lax.ppermute(first_row, "rows", [(i + 1, i) for i in range(slabs - 1)])
    backward = position >= count // 2
    turned = backward.astype(jnp.int32).reshape(1)
    args = (flags, low_flags, high_flags, turned, transfer, density, low_plane, high_plane, above, below)
    first = shade(0, 1, count, ray_step, *args)[0]
    rest = shade(1, count - 1, count, ray_step, *args)

    def own_piece(piece):
        at = jnp.where(backward, piece, count - 1 - piece)
        at = jnp.clip(at, 0, count - 1)
        other = lax.dynamic_index_in_dim(rest, jnp.maximum(at - 1, 0), 0, keepdims=False)
        return jnp.where(at == 0, first, other)

    front = back = None
    for step in range(count - 1):
        up_piece = own_piece(count - 1 - step + position) if step else first
        down_piece = own_piece(step + position - (count - 1)) if step else first
        if step:
            up_piece = blend_over(clear_unless(front, position > 0), up_piece)
            down_piece = blend_over(down_piece, clear_unless(back, position < count - 1))
        ups = [(i, i + 1) for i in range(step + 1)]
        downs = [(count - 1 - i, count - 2 - i) for i in range(step + 1)]
        front = lax.ppermute(up_piece, "depth", ups)
        back = lax.ppermute(down_piece, "depth", downs)
    merged = blend_over(own_piece(position), clear_unless(back, position < count - 1))
    merged = blend_over(clear_unless(front, position > 0), merged)
    return jnp.concatenate([merged[:3], 1.0 - merged[3:]], 0)


def solution(mesh):
    in_specs = (P("depth", "rows", None), P("depth", "rows", None), P())
    out_specs = P(None, "rows", "depth")
    return jax.shard_map(shards, mesh=mesh, in_specs=in_specs, out_specs=out_specs, check_vma=False)
```

```python
import functools
import jax
import jax.numpy as jnp
from jax import lax
from jax.experimental import pallas as pl
from jax.experimental.pallas import tpu as pltpu
from jax.sharding import PartitionSpec as P

OCCUPIED_MOST = 12
PAD = 8
ROWS_AT_ONCE = 16
HALVES = 2
LOG2_E = 1.4426950408889634
SMEM = pl.BlockSpec(memory_space=pltpu.SMEM)
VMEM = pl.BlockSpec(memory_space=pltpu.VMEM)
ANY = pl.BlockSpec(memory_space=pl.ANY)
HBM = pl.BlockSpec(memory_space=pltpu.HBM)


def pack_planes_kernel(width, flags, density, head, tail, sem):
    depth_cells, row_cells, _ = density.shape
    block_count = flags.shape[0]
    slots = min(OCCUPIED_MOST, block_count)

    def copies(block, slot):
        columns = pl.ds(pl.multiple_of(block * width, width), width)
        rows = pl.ds(pl.multiple_of(slot * row_cells, row_cells), row_cells)
        return (
            pltpu.make_async_copy(density.at[0, :, columns], head.at[rows, :], sem.at[0, slot]),
            pltpu.make_async_copy(density.at[depth_cells - 1, :, columns], tail.at[rows, :], sem.at[1, slot]),
        )

    def begin(block, slot):
        wanted = jnp.logical_and(flags[block] > 0, slot < slots)

        @pl.when(wanted)
        def _():
            for copy in copies(block, slot):
                copy.start()

        return slot + wanted.astype(jnp.int32)

    used = lax.fori_loop(0, block_count, begin, jnp.int32(0))
    lane = lax.broadcasted_iota(jnp.int32, (8, width), 1)
    row_of_flags = jnp.zeros((8, width), jnp.float32)
    for block in range(block_count):
        row_of_flags = jnp.where(lane == block, flags[block].astype(jnp.float32), row_of_flags)
    head[pl.ds(slots * row_cells, 8), :] = row_of_flags
    tail[pl.ds(slots * row_cells, 8), :] = row_of_flags

    def end(slot, carry):
        for copy in copies(0, slot):
            copy.wait()
        return carry

    lax.fori_loop(0, used, end, 0)


def pack_planes(density, flags, width):
    row_cells = density.shape[1]
    slots = min(OCCUPIED_MOST, flags.shape[0])
    plane = jax.ShapeDtypeStruct((slots * row_cells + 8, width), jnp.float32)
    return pl.pallas_call(
        functools.partial(pack_planes_kernel, width),
        out_shape=(plane, plane),
        in_specs=[SMEM, ANY],
        out_specs=[VMEM] * 2,
        scratch_shapes=[pltpu.SemaphoreType.DMA((2, slots))],
        name="pack_planes",
    )(flags, density)


def pack_rows_kernel(width, flags, density, first_row, last_row, top, bottom, sem):
    depth_cells, row_cells, _ = density.shape
    block_count = flags.shape[0]
    top_copy = pltpu.make_async_copy(density.at[:, 0:8, :], top, sem.at[0])
    bottom_copy = pltpu.make_async_copy(density.at[:, row_cells - 8 : row_cells, :], bottom, sem.at[1])
    top_copy.start()
    bottom_copy.start()
    top_copy.wait()
    bottom_copy.wait()

    def edge(block, carry):
        columns = pl.ds(pl.multiple_of(block * width, width), width)
        flag = flags[block].astype(jnp.float32)
        for z in range(depth_cells):
            first_row[pl.ds(z, 1), columns] = top[z, 0:1, columns] * flag
            last_row[pl.ds(z, 1), columns] = bottom[z, 7:8, columns] * flag
        return carry

    lax.fori_loop(0, block_count, edge, 0)


def pack_rows(density, flags, width):
    depth_cells, _, col_cells = density.shape
    row = jax.ShapeDtypeStruct((depth_cells, col_cells), jnp.float32)
    return pl.pallas_call(
        functools.partial(pack_rows_kernel, width),
        out_shape=(row, row),
        in_specs=[SMEM, ANY],
        out_specs=[VMEM] * 2,
        scratch_shapes=[
            pltpu.VMEM((depth_cells, 8, col_cells), jnp.float32),
            pltpu.VMEM((depth_cells, 8, col_cells), jnp.float32),
            pltpu.SemaphoreType.DMA((2,)),
        ],
        name="pack_rows",
    )(flags, density)


def shade_kernel(
    first_at,
    piece_total,
    width,
    ray_step,
    first_row,
    row_cells,
    flags,
    turned,
    transfer,
    density,
    low_plane,
    high_plane,
    above,
    below,
    *others,
):
    *earlier, out, vol, side_flags, block_sem, plane_sem, flag_sem = others
    depth_cells, all_rows, _ = density.shape
    before = PAD if first_row > 0 else 0
    after = PAD if first_row + row_cells < all_rows else 0
    block_count = flags.shape[0]
    piece_blocks = block_count // piece_total
    skipped = 1 if earlier else 0
    piece_count = out.shape[0] - skipped
    half_rows = out.shape[3]
    slots = min(OCCUPIED_MOST, block_count)
    own = piece_count * piece_blocks
    zero_slot = own + 2
    backward = turned[0] > 0
    first_piece = jnp.where(backward, first_at, piece_total - first_at - piece_count)
    first_block = first_piece * piece_blocks
    body = pl.ds(PAD, row_cells)

    def block_of(slot):
        return first_block + slot - 1

    def occupied(block):
        inside = jnp.logical_and(block >= 0, block < block_count)
        return jnp.logical_and(inside, flags[jnp.clip(block, 0, block_count - 1)] > 0)

    def block_copy(slot):
        block = jnp.clip(block_of(slot), 0, block_count - 1)
        columns = pl.ds(pl.multiple_of(block * width, width), width)
        rows = pl.ds(first_row - before, before + row_cells + after)
        window = pl.ds(PAD - before, before + row_cells + after)
        return pltpu.make_async_copy(
            density.at[:, rows, columns], vol.at[slot, pl.ds(1, depth_cells), window, :], block_sem.at[slot]
        )

    def low_copy(slot, rank):
        rows = pl.ds(pl.multiple_of(rank * all_rows + first_row, row_cells), row_cells)
        return pltpu.make_async_copy(low_plane.at[rows, :], vol.at[slot, 0, body, :], plane_sem.at[0, slot])

    def high_copy(slot, rank):
        rows = pl.ds(pl.multiple_of(rank * all_rows + first_row, row_cells), row_cells)
        return pltpu.make_async_copy(
            high_plane.at[rows, :], vol.at[slot, depth_cells + 1, body, :], plane_sem.at[1, slot]
        )

    def begin_block(slot, carry):
        @pl.when(occupied(block_of(slot)))
        def _():
            block_copy(slot).start()

        return carry

    flag_rows = pl.ds(slots * all_rows, 8)
    flag_copies = [
        pltpu.make_async_copy(plane.at[flag_rows, :], side_flags.at[side], flag_sem.at[side])
        for side, plane in enumerate((low_plane, high_plane))
    ]
    for copy in flag_copies:
        copy.start()
    lax.fori_loop(0, own + 2, begin_block, 0)
    for half, done in enumerate(earlier):
        out[0, half] = done[0, 0]
    for copy in flag_copies:
        copy.wait()

    def begin_plane(block, ranks):
        low_rank, high_rank = ranks
        slot = block - first_block + 1
        mine = jnp.logical_and(jnp.logical_and(slot >= 1, slot <= own), flags[block] > 0)
        low = side_flags[0, 0, block] > 0.5
        high = side_flags[1, 0, block] > 0.5

        @pl.when(jnp.logical_and(mine, low))
        def _():
            low_copy(slot, low_rank).start()

        @pl.when(jnp.logical_and(mine, high))
        def _():
            high_copy(slot, high_rank).start()

        return (low_rank + low.astype(jnp.int32), high_rank + high.astype(jnp.int32))

    lax.fori_loop(0, block_count, begin_plane, (jnp.int32(0), jnp.int32(0)))

    def clear(z, carry):
        vol[zero_slot, z, body, :] = jnp.zeros((row_cells, width), jnp.float32)
        return carry

    lax.fori_loop(1, depth_cells + 1, clear, 0)

    def arrive(slot):
        @pl.when(occupied(block_of(slot)))
        def _():
            block_copy(slot).wait()

    arrive(0)
    arrive(1)

    def visit(slot, carry):
        block = block_of(slot)
        piece = block // piece_blocks - first_piece
        place = skipped + jnp.where(backward, piece, piece_count - 1 - piece)
        columns = pl.ds(pl.multiple_of(lax.rem(block, piece_blocks) * width, width), width)
        arrive(slot + 1)

        @pl.when(jnp.logical_not(occupied(block)))
        def _():
            for half in range(out.shape[1]):
                for channel in range(4):
                    value = 1.0 if channel == 3 else 0.0
                    out[place, half, channel, :, columns] = jnp.full((half_rows, width), value, jnp.float32)

        @pl.when(occupied(block))
        def _():
            left = jnp.where(occupied(block - 1), slot - 1, zero_slot)
            right = jnp.where(occupied(block + 1), slot + 1, zero_slot)
            source = pl.ds(pl.multiple_of(block * width, width), width)
            for z in range(depth_cells):
                if not before:
                    vol[slot, z + 1, pl.ds(PAD - 1, 1), :] = above[pl.ds(z, 1), source]
                if not after:
                    vol[slot, z + 1, pl.ds(PAD + row_cells, 1), :] = below[pl.ds(z, 1), source]
            for side, plane_copy in enumerate((low_copy, high_copy)):
                near = side_flags[side, 0, block] > 0.5

                @pl.when(near)
                def _():
                    plane_copy(slot, 0).wait()

                @pl.when(jnp.logical_not(near))
                def _():
                    vol[slot, side * (depth_cells + 1), body, :] = jnp.zeros((row_cells, width), jnp.float32)

            march(slot, left, right, place, columns)

        return carry

    def march(slot, left, right, place, columns):
        rows_at_once = ROWS_AT_ONCE
        shape = (rows_at_once, width)
        lane = lax.broadcasted_iota(jnp.int32, shape, 1)
        at_first = lane == 0
        at_last = lane == width - 1
        slopes = [transfer[0, channel] * 0.5 for channel in range(3)]
        offsets = [transfer[1, channel] * 0.5 for channel in range(3)]
        decay_slope = transfer[0, 3] * LOG2_E
        decay_offset = transfer[1, 3] * LOG2_E

        def chunk(at, carry):
            start = pl.multiple_of(PAD + at * rows_at_once, 8)
            rows = pl.ds(start, rows_at_once)
            previous = vol[slot, 0, rows, :]
            center = vol[slot, 1, rows, :]
            transmit = jnp.ones(shape, jnp.float32)
            plain = jnp.zeros(shape, jnp.float32)
            tinted = [jnp.zeros(shape, jnp.float32) for _ in range(3)]
            for z in range(1, depth_cells + 1):
                following = vol[slot, z + 1, rows, :]
                diff_z = following - previous
                diff_y = vol[slot, z, pl.ds(start + 1, rows_at_once), :] - vol[slot, z, pl.ds(start - 1, rows_at_once), :]
                right_side = pltpu.roll(jnp.where(at_first, vol[right, z, rows, :], center), width - 1, 1)
                left_side = pltpu.roll(jnp.where(at_last, vol[left, z, rows, :], center), 1, 1)
                diff_x = right_side - left_side
                facing = jnp.abs(diff_x + 0.9375 * diff_y + 0.75 * diff_z)
                norm = lax.rsqrt(diff_x * diff_x + diff_y * diff_y + (diff_z * diff_z + 4.0))
                lighting = facing * norm + (0.3 / 0.448)
                soft = jnp.log(1.0 + jnp.exp2(decay_slope * center + decay_offset))
                passed = transmit * jnp.exp2((center * (-ray_step * LOG2_E)) * soft)
                weight = (transmit - passed) * lighting
                transmit = passed
                plain = plain + weight
                for channel in range(3):
                    tinted[channel] = tinted[channel] + weight * jnp.tanh(slopes[channel] * center + offsets[channel])
                previous, center = center, following
            half = at // (half_rows // rows_at_once)
            target = pl.ds(pl.multiple_of(at * rows_at_once - half * half_rows, 8), rows_at_once)
            for channel in range(3):
                out[place, half, channel, target, columns] = 0.224 * (plain + tinted[channel])
            out[place, half, 3, target, columns] = transmit
            return carry

        lax.fori_loop(0, row_cells // rows_at_once, chunk, 0)

    lax.fori_loop(1, own + 1, visit, 0)


def shade(first_at, piece_count, piece_total, ray_step, first_row, rows, halves, flags, turned, transfer, density, low_plane, high_plane, above, below, *earlier):
    depth_cells, _, col_cells = density.shape
    block_count = flags.shape[0]
    width = col_cells // block_count
    own = piece_count * (block_count // piece_total)
    cells = own * depth_cells * rows * width
    shape = (piece_count + (1 if earlier else 0), halves, 4, rows // halves, col_cells // piece_total)
    return pl.pallas_call(
        functools.partial(shade_kernel, first_at, piece_total, width, ray_step, first_row, rows),
        out_shape=jax.ShapeDtypeStruct(shape, jnp.float32),
        in_specs=[SMEM] * 3 + [ANY] * 3 + [VMEM] * (2 + len(earlier)),
        out_specs=VMEM,
        scratch_shapes=[
            pltpu.VMEM((own + 3, depth_cells + 2, rows + 2 * PAD, width), jnp.float32),
            pltpu.SMEM((2, 8, width), jnp.float32),
            pltpu.SemaphoreType.DMA((own + 2,)),
            pltpu.SemaphoreType.DMA((2, own + 2)),
            pltpu.SemaphoreType.DMA((2,)),
        ],
        compiler_params=pltpu.CompilerParams(vmem_limit_bytes=48 << 20),
        cost_estimate=pl.CostEstimate(flops=60 * cells, bytes_accessed=4 * cells, transcendentals=7 * cells),
        name=f"shade_{first_at}_{first_row}",
    )(flags, turned, transfer, density, low_plane, high_plane, above, below, *earlier)


def merge_kernel(half, table, pieces, front, back, up, down, own, sem):
    copies = [pltpu.make_async_copy(pieces.at[table[side], half], own.at[side], sem.at[side]) for side in range(2)]
    for copy in copies:
        copy.start()
    opening = jnp.where(table[2] > 0, front[3], 1.0)
    closing = jnp.where(table[3] > 0, back[3], 1.0)
    copies[0].wait()
    up[3] = opening * own[0, 3]
    for channel in range(3):
        up[channel] = front[channel] + opening * own[0, channel]
    copies[1].wait()
    passed = own[1, 3]
    down[3] = passed * closing
    for channel in range(3):
        down[channel] = own[1, channel] + passed * back[channel]


def merge(half, table, pieces, front, back):
    part = pieces.shape[2:]
    cells = part[0] * part[1] * part[2]
    return pl.pallas_call(
        functools.partial(merge_kernel, half),
        out_shape=(jax.ShapeDtypeStruct(part, jnp.float32),) * 2,
        in_specs=[SMEM, HBM, VMEM, VMEM],
        out_specs=[VMEM, VMEM],
        scratch_shapes=[pltpu.VMEM((2,) + part, jnp.float32), pltpu.SemaphoreType.DMA((2,))],
        compiler_params=pltpu.CompilerParams(vmem_limit_bytes=16 << 20),
        cost_estimate=pl.CostEstimate(flops=4 * cells, bytes_accessed=24 * cells, transcendentals=0),
        name="merge",
    )(table, pieces, front, back)


def finish_kernel(half, table, pieces, front, back, *others):
    image, own, made, sem = others[-4:]
    rows = pl.ds(half * made.shape[1], made.shape[1])
    load = pltpu.make_async_copy(pieces.at[table[0], half], own, sem.at[0])
    load.start()
    opening = jnp.where(table[2] > 0, front[3], 1.0)
    closing = jnp.where(table[3] > 0, back[3], 1.0)
    load.wait()
    passed = opening * own[3]
    for channel in range(3):
        made[channel] = front[channel] + opening * own[channel] + passed * back[channel]
    made[3] = 1.0 - passed * closing
    store = pltpu.make_async_copy(made, image.at[:, rows, :], sem.at[1])
    store.start()
    store.wait()


def finish(half, table, pieces, front, back, image):
    part = pieces.shape[2:]
    cells = part[0] * part[1] * part[2]
    started = [] if image is None else [image]
    return pl.pallas_call(
        functools.partial(finish_kernel, half),
        out_shape=jax.ShapeDtypeStruct((part[0], HALVES * part[1], part[2]), jnp.float32),
        in_specs=[SMEM, HBM, VMEM, VMEM] + [ANY] * len(started),
        out_specs=ANY,
        scratch_shapes=[pltpu.VMEM(part, jnp.float32), pltpu.VMEM(part, jnp.float32), pltpu.SemaphoreType.DMA((2,))],
        input_output_aliases={4: 0} if started else {},
        compiler_params=pltpu.CompilerParams(vmem_limit_bytes=16 << 20),
        cost_estimate=pl.CostEstimate(flops=4 * cells, bytes_accessed=16 * cells, transcendentals=0),
        name="finish",
    )(table, pieces, front, back, *started)


def shards(density, occupancy, transfer):
    depth_cells, row_cells, col_cells = density.shape
    flags = occupancy.reshape(-1)
    block_count = flags.shape[0]
    width = col_cells // block_count
    count = lax.axis_size("depth")
    slabs = lax.axis_size("rows")
    position = lax.axis_index("depth")
    ray_step = 2.0 / (depth_cells * count)
    later = [(i, i + 1) for i in range(count - 1)]
    sooner = [(i + 1, i) for i in range(count - 1)]

    head, tail = pack_planes(density, flags, width)
    low_plane = lax.ppermute(tail, "depth", later)
    high_plane = lax.ppermute(head, "depth", sooner)
    first_row, last_row = pack_rows(density, flags, width)
    above = lax.ppermute(last_row, "rows", [(i, i + 1) for i in range(slabs - 1)])
    below = lax.ppermute(first_row, "rows", [(i + 1, i) for i in range(slabs - 1)])
    backward = position >= count // 2
    turned = backward.astype(jnp.int32).reshape(1)
    args = (flags, turned, transfer, density, low_plane, high_plane, above, below)
    half_rows = row_cells // HALVES
    first = [shade(0, 1, count, ray_step, half * half_rows, half_rows, 1, *args) for half in range(HALVES)]
    pieces = shade(1, count - 1, count, ray_step, 0, row_cells, HALVES, *args, *first)

    def place(piece):
        return jnp.clip(jnp.where(backward, piece, count - 1 - piece), 0, count - 1)

    def table(up_piece, down_piece):
        sides = [position > 0, position < count - 1]
        return jnp.stack([place(up_piece), place(down_piece)] + [side.astype(jnp.int32) for side in sides])

    fronts, backs = [None] * HALVES, [None] * HALVES
    for step in range(count - 1):
        ups = [(i, i + 1) for i in range(step + 1)]
        downs = [(count - 1 - i, count - 2 - i) for i in range(step + 1)]
        apart = step + 1 < count - 2 - step
        step_table = table(count - 1 - step + position, step + position - (count - 1))
        for half in range(HALVES):
            if step:
                up, down = merge(half, step_table, pieces, fronts[half], backs[half])
            else:
                up = down = first[half][0, 0]
            if apart:
                sent = jnp.where(backward, down, up) if step else up
                fronts[half] = backs[half] = lax.ppermute(sent, "depth", ups + downs)
            else:
                fronts[half] = lax.ppermute(up, "depth", ups)
                backs[half] = lax.ppermute(down, "depth", downs)
    image = None
    final_table = table(position, position)
    for half in range(HALVES):
        image = finish(half, final_table, pieces, fronts[half], backs[half], image)
    return image


def solution(mesh):
    in_specs = (P("depth", "rows", None), P("depth", "rows", None), P())
    out_specs = P(None, "rows", "depth")
    return jax.shard_map(shards, mesh=mesh, in_specs=in_specs, out_specs=out_specs, check_vma=False)
```

```python
import functools
import jax
import jax.numpy as jnp
from jax import lax
from jax.experimental import pallas as pl
from jax.experimental.pallas import tpu as pltpu
from jax.sharding import PartitionSpec as P

OCCUPIED_MOST = 12
PAD = 8
ROWS_AT_ONCE = 32
HALVES = 2
LOG2_E = 1.4426950408889634
SMEM = pl.BlockSpec(memory_space=pltpu.SMEM)
VMEM = pl.BlockSpec(memory_space=pltpu.VMEM)
ANY = pl.BlockSpec(memory_space=pl.ANY)


def pack_planes_kernel(width, flags, even, density, outer, inner, sem):
    depth_cells, row_cells, _ = density.shape
    block_count = flags.shape[0]
    slots = min(OCCUPIED_MOST, block_count)
    outer_plane = jnp.where(even[0] > 0, depth_cells - 1, 0)
    inner_plane = depth_cells - 1 - outer_plane

    def copies(block, slot):
        columns = pl.ds(pl.multiple_of(block * width, width), width)
        rows = pl.ds(pl.multiple_of(slot * row_cells, row_cells), row_cells)
        return (
            pltpu.make_async_copy(density.at[outer_plane, :, columns], outer.at[rows, :], sem.at[0, slot]),
            pltpu.make_async_copy(density.at[inner_plane, :, columns], inner.at[rows, :], sem.at[1, slot]),
        )

    def begin(block, slot):
        wanted = jnp.logical_and(flags[block] > 0, slot < slots)

        @pl.when(wanted)
        def _():
            for copy in copies(block, slot):
                copy.start()

        return slot + wanted.astype(jnp.int32)

    used = lax.fori_loop(0, block_count, begin, jnp.int32(0))
    lane = lax.broadcasted_iota(jnp.int32, (8, width), 1)
    row_of_flags = jnp.zeros((8, width), jnp.float32)
    for block in range(block_count):
        row_of_flags = jnp.where(lane == block, flags[block].astype(jnp.float32), row_of_flags)
    outer[pl.ds(slots * row_cells, 8), :] = row_of_flags
    inner[pl.ds(slots * row_cells, 8), :] = row_of_flags

    def end(slot, carry):
        for copy in copies(0, slot):
            copy.wait()
        return carry

    lax.fori_loop(0, used, end, 0)


def pack_planes(density, flags, even, width):
    row_cells = density.shape[1]
    slots = min(OCCUPIED_MOST, flags.shape[0])
    plane = jax.ShapeDtypeStruct((slots * row_cells + 8, width), jnp.float32)
    return pl.pallas_call(
        functools.partial(pack_planes_kernel, width),
        out_shape=(plane, plane),
        in_specs=[SMEM, SMEM, ANY],
        out_specs=[VMEM] * 2,
        scratch_shapes=[pltpu.SemaphoreType.DMA((2, slots))],
        name="pack_planes",
    )(flags, even, density)


def pack_rows_kernel(width, flags, density, first_row, last_row, top, bottom, sem):
    depth_cells, row_cells, _ = density.shape
    block_count = flags.shape[0]
    top_copy = pltpu.make_async_copy(density.at[:, 0:8, :], top, sem.at[0])
    bottom_copy = pltpu.make_async_copy(density.at[:, row_cells - 8 : row_cells, :], bottom, sem.at[1])
    top_copy.start()
    bottom_copy.start()
    top_copy.wait()
    bottom_copy.wait()

    def edge(block, carry):
        columns = pl.ds(pl.multiple_of(block * width, width), width)
        flag = flags[block].astype(jnp.float32)
        for z in range(depth_cells):
            first_row[pl.ds(z, 1), columns] = top[z, 0:1, columns] * flag
            last_row[pl.ds(z, 1), columns] = bottom[z, 7:8, columns] * flag
        return carry

    lax.fori_loop(0, block_count, edge, 0)


def pack_rows(density, flags, width):
    depth_cells, _, col_cells = density.shape
    row = jax.ShapeDtypeStruct((depth_cells, col_cells), jnp.float32)
    return pl.pallas_call(
        functools.partial(pack_rows_kernel, width),
        out_shape=(row, row),
        in_specs=[SMEM, ANY],
        out_specs=[VMEM] * 2,
        scratch_shapes=[
            pltpu.VMEM((depth_cells, 8, col_cells), jnp.float32),
            pltpu.VMEM((depth_cells, 8, col_cells), jnp.float32),
            pltpu.SemaphoreType.DMA((2,)),
        ],
        name="pack_rows",
    )(flags, density)


def shade_kernel(mode, first_at, piece_total, width, ray_step, first_row, flags, place, transfer, density, above, below, *others):
    planes = others[: 0 if mode == "core" else 2]
    core = others[2] if mode == "edge" else None
    out, vol, side_flags, block_sem, plane_sem, flag_sem = others[-6:]
    depth_cells, all_rows, _ = density.shape
    piece_count, halves, _, half_rows, _ = out.shape
    row_cells = halves * half_rows
    before = PAD if first_row > 0 else 0
    after = PAD if first_row + row_cells < all_rows else 0
    block_count = flags.shape[0]
    piece_blocks = block_count // piece_total
    slots = min(OCCUPIED_MOST, block_count)
    own = piece_count * piece_blocks
    zero_slot = own + 2
    backward = place[0] > 0
    even = place[1] > 0
    first_piece = jnp.where(backward, first_at, piece_total - first_at - piece_count)
    first_block = first_piece * piece_blocks
    body = pl.ds(PAD, row_cells)
    if mode == "edge":
        held = [(1, 0, 2), (3, depth_cells - 2, 2)]
        runs = [[(1, 0)], [(4, depth_cells - 1)]]
        low_at, high_at = 0, 5
    else:
        held = [(1, 0, depth_cells)]
        trim = 1 if mode == "core" else 0
        runs = [[(z + 1, z) for z in range(trim, depth_cells - trim)]]
        low_at, high_at = 0, depth_cells + 1

    def block_of(slot):
        return first_block + slot - 1

    def occupied(block):
        inside = jnp.logical_and(block >= 0, block < block_count)
        return jnp.logical_and(inside, flags[jnp.clip(block, 0, block_count - 1)] > 0)

    def block_copies(slot):
        block = jnp.clip(block_of(slot), 0, block_count - 1)
        columns = pl.ds(pl.multiple_of(block * width, width), width)
        rows = pl.ds(first_row - before, before + row_cells + after)
        window = pl.ds(PAD - before, before + row_cells + after)
        return [
            pltpu.make_async_copy(
                density.at[pl.ds(z, count), rows, columns], vol.at[slot, pl.ds(at, count), window, :], block_sem.at[part, slot]
            )
            for part, (at, z, count) in enumerate(held)
        ]

    def plane_copy(side, which, slot, rank):
        rows = pl.ds(pl.multiple_of(rank * all_rows + first_row, row_cells), row_cells)
        at = high_at if side else low_at
        return pltpu.make_async_copy(planes[which].at[rows, :], vol.at[slot, at, body, :], plane_sem.at[side, slot])

    flag_rows = pl.ds(slots * all_rows, 8)
    flag_copies = [
        pltpu.make_async_copy(plane.at[flag_rows, :], side_flags.at[which], flag_sem.at[which])
        for which, plane in enumerate(planes)
    ]
    for copy in flag_copies:
        copy.start()

    def begin_block(slot, carry):
        @pl.when(occupied(block_of(slot)))
        def _():
            for copy in block_copies(slot):
                copy.start()

        return carry

    lax.fori_loop(0, own + 2, begin_block, 0)
    for copy in flag_copies:
        copy.wait()

    def near(side, block):
        which = jnp.where(even, 1 - side, side)
        return side_flags[which, 0, block] > 0.5

    def begin_plane(block, ranks):
        slot = block - first_block + 1
        mine = jnp.logical_and(jnp.logical_and(slot >= 1, slot <= own), flags[block] > 0)
        after_this = []
        for side in range(2):
            close = near(side, block)
            wanted = jnp.logical_and(mine, close)
            for which in range(2):
                chosen = even if which != side else jnp.logical_not(even)

                @pl.when(jnp.logical_and(wanted, chosen))
                def _():
                    plane_copy(side, which, slot, ranks[side]).start()

            after_this.append(ranks[side] + close.astype(jnp.int32))
        return tuple(after_this)

    if planes:
        lax.fori_loop(0, block_count, begin_plane, (jnp.int32(0), jnp.int32(0)))
    for run in runs:
        for z, _ in run:
            vol[zero_slot, z, body, :] = jnp.zeros((row_cells, width), jnp.float32)

    def arrive(slot):
        @pl.when(occupied(block_of(slot)))
        def _():
            for copy in block_copies(slot):
                copy.wait()

    arrive(0)
    arrive(1)

    def visit(slot, carry):
        block = block_of(slot)
        piece = block // piece_blocks - first_piece
        at = jnp.where(backward, piece, piece_count - 1 - piece)
        columns = pl.ds(pl.multiple_of(lax.rem(block, piece_blocks) * width, width), width)
        arrive(slot + 1)

        @pl.when(jnp.logical_not(occupied(block)))
        def _():
            for half in range(halves):
                for channel in range(4):
                    value = 1.0 if channel == 3 else 0.0
                    out[at, half, channel, :, columns] = jnp.full((half_rows, width), value, jnp.float32)

        @pl.when(occupied(block))
        def _():
            left = jnp.where(occupied(block - 1), slot - 1, zero_slot)
            right = jnp.where(occupied(block + 1), slot + 1, zero_slot)
            source = pl.ds(pl.multiple_of(block * width, width), width)
            for run in runs:
                for z, depth in run:
                    if not before:
                        vol[slot, z, pl.ds(PAD - 1, 1), :] = above[pl.ds(depth, 1), source]
                    if not after:
                        vol[slot, z, pl.ds(PAD + row_cells, 1), :] = below[pl.ds(depth, 1), source]
            for side in range(2 if planes else 0):
                close = near(side, block)

                @pl.when(close)
                def _():
                    plane_copy(side, 0, slot, 0).wait()

                @pl.when(jnp.logical_not(close))
                def _():
                    vol[slot, high_at if side else low_at, body, :] = jnp.zeros((row_cells, width), jnp.float32)

            march(slot, left, right, at, columns)

        return carry

    def march(slot, left, right, piece_at, columns):
        rows_at_once = min(ROWS_AT_ONCE, half_rows)
        shape = (rows_at_once, width)
        lane = lax.broadcasted_iota(jnp.int32, shape, 1)
        at_first = lane == 0
        at_last = lane == width - 1
        slopes = [transfer[0, channel] * 0.5 for channel in range(3)]
        offsets = [transfer[1, channel] * 0.5 for channel in range(3)]
        decay_slope = transfer[0, 3] * LOG2_E
        decay_offset = transfer[1, 3] * LOG2_E

        def shaded(run, start):
            rows = pl.ds(start, rows_at_once)
            previous = vol[slot, run[0][0] - 1, rows, :]
            center = vol[slot, run[0][0], rows, :]
            transmit = jnp.ones(shape, jnp.float32)
            plain = jnp.zeros(shape, jnp.float32)
            tinted = [plain] * 3
            for z, _ in run:
                following = vol[slot, z + 1, rows, :]
                diff_z = following - previous
                diff_y = vol[slot, z, pl.ds(start + 1, rows_at_once), :] - vol[slot, z, pl.ds(start - 1, rows_at_once), :]
                right_side = pltpu.roll(jnp.where(at_first, vol[right, z, rows, :], center), width - 1, 1)
                left_side = pltpu.roll(jnp.where(at_last, vol[left, z, rows, :], center), 1, 1)
                diff_x = right_side - left_side
                facing = jnp.abs(diff_x + 0.9375 * diff_y + 0.75 * diff_z)
                norm = lax.rsqrt(diff_x * diff_x + diff_y * diff_y + (diff_z * diff_z + 4.0))
                lighting = facing * norm + (0.3 / 0.448)
                soft = lax.log2(1.0 + jnp.exp2(decay_slope * center + decay_offset))
                passed = transmit * jnp.exp2((center * -ray_step) * soft)
                weight = (transmit - passed) * lighting
                transmit = passed
                plain = plain + weight
                tinted = [
                    tinted[channel] + weight * jnp.tanh(slopes[channel] * center + offsets[channel]) for channel in range(3)
                ]
                previous, center = center, following
            return [0.224 * (plain + tinted[channel]) for channel in range(3)], transmit

        def chunk(at, carry):
            start = pl.multiple_of(PAD + at * rows_at_once, 8)
            half = at // (half_rows // rows_at_once)
            target = pl.ds(pl.multiple_of(at * rows_at_once - half * half_rows, 8), rows_at_once)
            colors, transmit = shaded(runs[0], start)
            if mode == "edge":
                middle_half = first_row // half_rows
                inner = core[0, middle_half, 3, target, columns]
                back_colors, back_transmit = shaded(runs[1], start)
                colors = [
                    colors[channel] + transmit * (core[0, middle_half, channel, target, columns] + inner * back_colors[channel])
                    for channel in range(3)
                ]
                transmit = transmit * inner * back_transmit
            for channel in range(3):
                out[piece_at, half, channel, target, columns] = colors[channel]
            out[piece_at, half, 3, target, columns] = transmit
            return carry

        lax.fori_loop(0, row_cells // rows_at_once, chunk, 0)

    lax.fori_loop(1, own + 1, visit, 0)


def shade(mode, first_at, piece_count, piece_total, ray_step, first_row, rows, flags, place, transfer, density, above, below, *others):
    depth_cells, all_rows, col_cells = density.shape
    block_count = flags.shape[0]
    width = col_cells // block_count
    own = piece_count * (block_count // piece_total)
    half_rows = all_rows // HALVES
    depth = 2 if mode == "edge" else depth_cells
    cells = own * depth * rows * width
    held = 6 if mode == "edge" else depth_cells + 2
    shape = (piece_count, rows // half_rows, 4, half_rows, col_cells // piece_total)
    extra = {"core": [], "edge": [ANY, ANY, VMEM], "full": [ANY, ANY]}[mode]
    return pl.pallas_call(
        functools.partial(shade_kernel, mode, first_at, piece_total, width, ray_step, first_row),
        out_shape=jax.ShapeDtypeStruct(shape, jnp.float32),
        in_specs=[SMEM] * 3 + [ANY] + [VMEM] * 2 + extra + [SMEM] * (len(others) - len(extra)),
        out_specs=VMEM,
        scratch_shapes=[
            pltpu.VMEM((own + 3, held, rows + 2 * PAD, width), jnp.float32),
            pltpu.SMEM((2, 8, width), jnp.float32),
            pltpu.SemaphoreType.DMA((2, own + 2)),
            pltpu.SemaphoreType.DMA((2, own + 2)),
            pltpu.SemaphoreType.DMA((2,)),
        ],
        compiler_params=pltpu.CompilerParams(vmem_limit_bytes=48 << 20),
        cost_estimate=pl.CostEstimate(flops=60 * cells, bytes_accessed=4 * cells, transcendentals=7 * cells),
        name=f"shade_{mode}_{first_at}_{first_row}",
    )(flags, place, transfer, density, above, below, *others)


def fetch(half, at, pieces, own, sem):
    at = jnp.minimum(at, sum(piece.shape[0] for piece in pieces) - 1)
    first = 0
    for piece in pieces:
        for local in range(piece.shape[0]):

            @pl.when(at == first)
            def _():
                pltpu.make_async_copy(piece.at[local, half if piece.shape[1] > 1 else 0], own, sem).start()

            first += 1
    return pltpu.make_async_copy(pieces[0].at[0, 0], own, sem)


def merge_kernel(half, table, front, back, *others):
    pieces = others[:-5]
    up, down, token, own, sem = others[-5:]
    copies = [fetch(half, table[side], pieces, own.at[side], sem.at[side]) for side in range(2)]
    opening = jnp.where(table[2] > 0, front[3], 1.0)
    closing = jnp.where(table[3] > 0, back[3], 1.0)
    token[0] = table[0]
    copies[0].wait()
    up[3] = opening * own[0, 3]
    for channel in range(3):
        up[channel] = front[channel] + opening * own[0, channel]
    copies[1].wait()
    passed = own[1, 3]
    down[3] = passed * closing
    for channel in range(3):
        down[channel] = own[1, channel] + passed * back[channel]


def merge(half, table, pieces, front, back):
    part = pieces[0].shape[2:]
    cells = part[0] * part[1] * part[2]
    return pl.pallas_call(
        functools.partial(merge_kernel, half),
        out_shape=(jax.ShapeDtypeStruct(part, jnp.float32),) * 2 + (jax.ShapeDtypeStruct((1,), jnp.int32),),
        in_specs=[SMEM, VMEM, VMEM] + [ANY] * len(pieces),
        out_specs=[VMEM, VMEM, SMEM],
        scratch_shapes=[pltpu.VMEM((2,) + part, jnp.float32), pltpu.SemaphoreType.DMA((2,))],
        compiler_params=pltpu.CompilerParams(vmem_limit_bytes=16 << 20),
        cost_estimate=pl.CostEstimate(flops=4 * cells, bytes_accessed=24 * cells, transcendentals=0),
        name="merge",
    )(table, front, back, *pieces)


def finish_kernel(half, table, front, back, *others):
    image, own, made, sem = others[-4:]
    pieces = others[:-5] if half else others[:-4]
    rows = pl.ds(half * made.shape[1], made.shape[1])
    load = fetch(half, table[0], pieces, own, sem.at[0])
    opening = jnp.where(table[2] > 0, front[3], 1.0)
    closing = jnp.where(table[3] > 0, back[3], 1.0)
    load.wait()
    passed = opening * own[3]
    for channel in range(3):
        made[channel] = front[channel] + opening * own[channel] + passed * back[channel]
    made[3] = 1.0 - passed * closing
    store = pltpu.make_async_copy(made, image.at[:, rows, :], sem.at[1])
    store.start()
    store.wait()


def finish(half, table, pieces, front, back, image):
    part = pieces[0].shape[2:]
    cells = part[0] * part[1] * part[2]
    started = [] if image is None else [image]
    return pl.pallas_call(
        functools.partial(finish_kernel, half),
        out_shape=jax.ShapeDtypeStruct((part[0], HALVES * part[1], part[2]), jnp.float32),
        in_specs=[SMEM, VMEM, VMEM] + [ANY] * (len(pieces) + len(started)),
        out_specs=ANY,
        scratch_shapes=[pltpu.VMEM(part, jnp.float32), pltpu.VMEM(part, jnp.float32), pltpu.SemaphoreType.DMA((2,))],
        input_output_aliases={3 + len(pieces): 0} if started else {},
        compiler_params=pltpu.CompilerParams(vmem_limit_bytes=16 << 20),
        cost_estimate=pl.CostEstimate(flops=4 * cells, bytes_accessed=16 * cells, transcendentals=0),
        name="finish",
    )(table, front, back, *pieces, *started)


def shards(density, occupancy, transfer):
    depth_cells, row_cells, col_cells = density.shape
    flags = occupancy.reshape(-1)
    block_count = flags.shape[0]
    width = col_cells // block_count
    count = lax.axis_size("depth")
    slabs = lax.axis_size("rows")
    position = lax.axis_index("depth")
    ray_step = 2.0 / (depth_cells * count)
    backward = position >= count // 2
    even = lax.rem(position, 2) == 0
    place = jnp.stack([backward.astype(jnp.int32), even.astype(jnp.int32)])

    def pairs(start):
        found = []
        for low in range(start, count - 1, 2):
            found += [(low, low + 1), (low + 1, low)]
        return found

    outer, inner = pack_planes(density, flags, even.astype(jnp.int32).reshape(1), width)
    outer_plane = lax.ppermute(outer, "depth", pairs(0))
    inner_plane = lax.ppermute(inner, "depth", pairs(1)) if count > 2 else jnp.zeros_like(inner)
    first_row, last_row = pack_rows(density, flags, width)
    above = lax.ppermute(last_row, "rows", [(i, i + 1) for i in range(slabs - 1)])
    below = lax.ppermute(first_row, "rows", [(i + 1, i) for i in range(slabs - 1)])
    args = (flags, place, transfer, density, above, below)
    half_rows = row_cells // HALVES
    core = shade("core", 0, 1, count, ray_step, 0, row_cells, *args)
    first = [
        shade("edge", 0, 1, count, ray_step, half * half_rows, half_rows, *args, outer_plane, inner_plane, core)
        for half in range(HALVES)
    ]
    second = shade("full", 1, 1, count, ray_step, 0, row_cells, *args, outer_plane, inner_plane)
    rest = None

    def rank(piece):
        return jnp.clip(jnp.where(backward, piece, count - 1 - piece), 0, count - 1)

    def table(up_piece, down_piece):
        sides = [position > 0, position < count - 1]
        return jnp.stack([rank(up_piece), rank(down_piece)] + [side.astype(jnp.int32) for side in sides])

    fronts, backs = [None] * HALVES, [None] * HALVES
    token = None
    for step in range(count - 1):
        ups = [(i, i + 1) for i in range(step + 1)]
        downs = [(count - 1 - i, count - 2 - i) for i in range(step + 1)]
        apart = step + 1 < count - 2 - step
        step_table = table(count - 1 - step + position, step + position - (count - 1))
        if step == 2:
            rest = shade("full", 2, count - 2, count, ray_step, 0, row_cells, *args, outer_plane, inner_plane, token)
        for half in range(HALVES):
            if step:
                pieces = [first[half], second] + ([rest] if rest is not None else [])
                up, down, token = merge(half, step_table, pieces, fronts[half], backs[half])
            else:
                up = down = first[half][0, 0]
            if apart:
                sent = jnp.where(backward, down, up) if step else up
                fronts[half] = backs[half] = lax.ppermute(sent, "depth", ups + downs)
            else:
                fronts[half] = lax.ppermute(up, "depth", ups)
                backs[half] = lax.ppermute(down, "depth", downs)
    image = None
    final_table = table(position, position)
    for half in range(HALVES):
        image = finish(half, final_table, [first[half], second, rest], fronts[half], backs[half], image)
    return image


def solution(mesh):
    in_specs = (P("depth", "rows", None), P("depth", "rows", None), P())
    out_specs = P(None, "rows", "depth")
    return jax.shard_map(shards, mesh=mesh, in_specs=in_specs, out_specs=out_specs, check_vma=False)
```

```python
import functools
import jax
import jax.numpy as jnp
from jax import lax
from jax.experimental import pallas as pl
from jax.experimental.pallas import tpu as pltpu
from jax.sharding import PartitionSpec as P

OCCUPIED_MOST = 12
PAD = 8
ROWS_AT_ONCE = 32
HALVES = 2
LOG2_E = 1.4426950408889634
SMEM = pl.BlockSpec(memory_space=pltpu.SMEM)
VMEM = pl.BlockSpec(memory_space=pltpu.VMEM)
ANY = pl.BlockSpec(memory_space=pl.ANY)


def pack_planes_kernel(width, flags, even, density, outer, inner, sem):
    depth_cells, row_cells, _ = density.shape
    block_count = flags.shape[0]
    slots = min(OCCUPIED_MOST, block_count)
    outer_plane = jnp.where(even[0] > 0, depth_cells - 1, 0)
    inner_plane = depth_cells - 1 - outer_plane

    def copies(block, slot):
        columns = pl.ds(pl.multiple_of(block * width, width), width)
        rows = pl.ds(pl.multiple_of(slot * row_cells, row_cells), row_cells)
        return (
            pltpu.make_async_copy(density.at[outer_plane, :, columns], outer.at[rows, :], sem.at[0, slot]),
            pltpu.make_async_copy(density.at[inner_plane, :, columns], inner.at[rows, :], sem.at[1, slot]),
        )

    def begin(block, slot):
        wanted = jnp.logical_and(flags[block] > 0, slot < slots)

        @pl.when(wanted)
        def _():
            for copy in copies(block, slot):
                copy.start()

        return slot + wanted.astype(jnp.int32)

    used = lax.fori_loop(0, block_count, begin, jnp.int32(0))
    lane = lax.broadcasted_iota(jnp.int32, (8, width), 1)
    row_of_flags = jnp.zeros((8, width), jnp.float32)
    for block in range(block_count):
        row_of_flags = jnp.where(lane == block, flags[block].astype(jnp.float32), row_of_flags)
    outer[pl.ds(slots * row_cells, 8), :] = row_of_flags
    inner[pl.ds(slots * row_cells, 8), :] = row_of_flags

    def end(slot, carry):
        for copy in copies(0, slot):
            copy.wait()
        return carry

    lax.fori_loop(0, used, end, 0)


def pack_planes(density, flags, even, width):
    row_cells = density.shape[1]
    slots = min(OCCUPIED_MOST, flags.shape[0])
    plane = jax.ShapeDtypeStruct((slots * row_cells + 8, width), jnp.float32)
    return pl.pallas_call(
        functools.partial(pack_planes_kernel, width),
        out_shape=(plane, plane),
        in_specs=[SMEM, SMEM, ANY],
        out_specs=[VMEM] * 2,
        scratch_shapes=[pltpu.SemaphoreType.DMA((2, slots))],
        compiler_params=pltpu.CompilerParams(vmem_limit_bytes=50 << 20),
        name="pack_planes",
    )(flags, even, density)


def pack_rows_kernel(width, flags, density, first_row, last_row, top, bottom, sem):
    depth_cells, row_cells, _ = density.shape
    block_count = flags.shape[0]
    top_copy = pltpu.make_async_copy(density.at[:, 0:8, :], top, sem.at[0])
    bottom_copy = pltpu.make_async_copy(density.at[:, row_cells - 8 : row_cells, :], bottom, sem.at[1])
    top_copy.start()
    bottom_copy.start()
    top_copy.wait()
    bottom_copy.wait()

    def edge(block, carry):
        columns = pl.ds(pl.multiple_of(block * width, width), width)
        flag = flags[block].astype(jnp.float32)
        for z in range(depth_cells):
            first_row[pl.ds(z, 1), columns] = top[z, 0:1, columns] * flag
            last_row[pl.ds(z, 1), columns] = bottom[z, 7:8, columns] * flag
        return carry

    lax.fori_loop(0, block_count, edge, 0)


def pack_rows(density, flags, width):
    depth_cells, _, col_cells = density.shape
    row = jax.ShapeDtypeStruct((depth_cells, col_cells), jnp.float32)
    return pl.pallas_call(
        functools.partial(pack_rows_kernel, width),
        out_shape=(row, row),
        in_specs=[SMEM, ANY],
        out_specs=[VMEM] * 2,
        scratch_shapes=[
            pltpu.VMEM((depth_cells, 8, col_cells), jnp.float32),
            pltpu.VMEM((depth_cells, 8, col_cells), jnp.float32),
            pltpu.SemaphoreType.DMA((2,)),
        ],
        compiler_params=pltpu.CompilerParams(vmem_limit_bytes=50 << 20),
        name="pack_rows",
    )(flags, density)


def shade_kernel(mode, piece_total, width, ray_step, flags, place, transfer, density, above, below, *others):
    plane_count = {"core": 0, "edge": 1, "full": 2}[mode]
    planes = others[:plane_count]
    others = others[plane_count:]
    if mode == "edge":
        core, *others = others
    *outs, vol, side_flags, block_sem, plane_sem, flag_sem = others
    depth_cells, row_cells, _ = density.shape
    block_count = flags.shape[0]
    piece_blocks = block_count // piece_total
    slots = min(OCCUPIED_MOST, block_count)
    backward = place[0] > 0
    even = place[1] > 0
    ending = place[2] > 0
    own = block_count if mode == "full" else piece_blocks
    zero_slot = own + 2
    first_piece = jnp.where(backward, 0, piece_total - 1)
    first_block = 0 if mode == "full" else first_piece * piece_blocks
    body = pl.ds(PAD, row_cells)
    half_rows = row_cells // HALVES
    if mode == "edge":
        held = [(1, 0, 2), (3, depth_cells - 2, 2)]
        runs = [[(1, 0)], [(4, depth_cells - 1)]]
        low_at, high_at = 0, 5
    else:
        held = [(1, 0, depth_cells)]
        trim = 1 if mode == "core" else 0
        runs = [[(z + 1, z) for z in range(trim, depth_cells - trim)]]
        low_at, high_at = 0, depth_cells + 1

    def put(piece_at, half, channel, rows, columns, value):
        if mode == "edge":
            outs[half][channel, rows, columns] = value
        else:
            outs[0][piece_at, half, channel, rows, columns] = value

    def block_of(slot):
        return first_block + slot - 1

    def occupied(block):
        inside = jnp.logical_and(block >= 0, block < block_count)
        return jnp.logical_and(inside, flags[jnp.clip(block, 0, block_count - 1)] > 0)

    def done_before(block):
        piece = jnp.clip(block, 0, block_count - 1) // piece_blocks
        return jnp.logical_and(ending, piece == first_piece) if mode == "full" else False

    def needed(block):
        if mode != "full":
            return occupied(block)
        idle = jnp.logical_and(done_before(block - 1), jnp.logical_and(done_before(block), done_before(block + 1)))
        return jnp.logical_and(occupied(block), jnp.logical_not(idle))

    def block_copies(slot):
        block = jnp.clip(block_of(slot), 0, block_count - 1)
        columns = pl.ds(pl.multiple_of(block * width, width), width)
        return [
            pltpu.make_async_copy(
                density.at[pl.ds(z, count), :, columns], vol.at[slot, pl.ds(at, count), body, :], block_sem.at[part, slot]
            )
            for part, (at, z, count) in enumerate(held)
        ]

    def plane_copy(side, which, slot, rank):
        rows = pl.ds(pl.multiple_of(rank * row_cells, row_cells), row_cells)
        at = high_at if side else low_at
        return pltpu.make_async_copy(planes[which].at[rows, :], vol.at[slot, at, body, :], plane_sem.at[side, slot])

    def near(side, block):
        if mode == "edge":
            return jnp.logical_and(backward if side == 0 else jnp.logical_not(backward), side_flags[0, 0, block] > 0.5)
        which = jnp.where(even, 1 - side, side)
        return side_flags[which, 0, block] > 0.5

    def begin_block(slot, carry):
        @pl.when(needed(block_of(slot)))
        def _():
            for copy in block_copies(slot):
                copy.start()

        return carry

    def begin_plane(block, ranks):
        mine = jnp.logical_and(flags[block] > 0, jnp.logical_not(done_before(block)))
        after_this = []
        for side in range(2):
            close = near(side, block)
            wanted = jnp.logical_and(mine, close)
            for which in range(2):
                chosen = even if which != side else jnp.logical_not(even)

                @pl.when(jnp.logical_and(wanted, chosen))
                def _():
                    plane_copy(side, which, block + 1, ranks[side]).start()

            after_this.append(ranks[side] + close.astype(jnp.int32))
        return tuple(after_this)

    def arrive(slot):
        @pl.when(needed(block_of(slot)))
        def _():
            for copy in block_copies(slot):
                copy.wait()

    def visit(slot, carry):
        block = block_of(slot)
        piece = block // piece_blocks
        at = jnp.where(backward, piece, piece_total - 1 - piece) if mode == "full" else 0
        columns = pl.ds(pl.multiple_of(lax.rem(block, piece_blocks) * width, width), width)
        arrive(slot + 1)

        @pl.when(jnp.logical_not(occupied(block)))
        def _():
            for half in range(HALVES):
                for channel in range(4):
                    value = 1.0 if channel == 3 else 0.0
                    put(at, half, channel, slice(None), columns, jnp.full((half_rows, width), value, jnp.float32))

        @pl.when(jnp.logical_and(occupied(block), jnp.logical_not(done_before(block))))
        def _():
            left = jnp.where(occupied(block - 1), slot - 1, zero_slot)
            right = jnp.where(occupied(block + 1), slot + 1, zero_slot)
            source = pl.ds(pl.multiple_of(block * width, width), width)
            for run in runs:
                for z, depth in run:
                    vol[slot, z, pl.ds(PAD - 1, 1), :] = above[pl.ds(depth, 1), source]
                    vol[slot, z, pl.ds(PAD + row_cells, 1), :] = below[pl.ds(depth, 1), source]
            for side in range(2 if planes else 0):
                close = near(side, block)
                side_at = high_at if side else low_at

                @pl.when(close)
                def _():
                    if mode == "full":
                        plane_copy(side, 0, slot, 0).wait()
                    else:
                        rank = lax.fori_loop(
                            0, block, lambda i, found: found + jnp.where(side_flags[0, 0, i] > 0.5, 1, 0), jnp.int32(0)
                        )
                        rows = pl.ds(pl.multiple_of(rank * row_cells, row_cells), row_cells)
                        vol[slot, side_at, body, :] = planes[0][rows, :]

                @pl.when(jnp.logical_not(close))
                def _():
                    vol[slot, side_at, body, :] = jnp.zeros((row_cells, width), jnp.float32)

            march(slot, left, right, at, columns)

        return carry

    def march(slot, left, right, piece_at, columns):
        rows_at_once = min(ROWS_AT_ONCE, half_rows)
        shape = (rows_at_once, width)
        lane = lax.broadcasted_iota(jnp.int32, shape, 1)
        at_first = lane == 0
        at_last = lane == width - 1
        slopes = [transfer[0, channel] * 0.5 for channel in range(3)]
        offsets = [transfer[1, channel] * 0.5 for channel in range(3)]
        decay_slope = transfer[0, 3] * LOG2_E
        decay_offset = transfer[1, 3] * LOG2_E

        def shaded(run, start):
            rows = pl.ds(start, rows_at_once)
            previous = vol[slot, run[0][0] - 1, rows, :]
            center = vol[slot, run[0][0], rows, :]
            transmit = jnp.ones(shape, jnp.float32)
            plain = jnp.zeros(shape, jnp.float32)
            tinted = [plain] * 3
            for z, _ in run:
                following = vol[slot, z + 1, rows, :]
                diff_z = following - previous
                diff_y = vol[slot, z, pl.ds(start + 1, rows_at_once), :] - vol[slot, z, pl.ds(start - 1, rows_at_once), :]
                right_side = pltpu.roll(jnp.where(at_first, vol[right, z, rows, :], center), width - 1, 1)
                left_side = pltpu.roll(jnp.where(at_last, vol[left, z, rows, :], center), 1, 1)
                diff_x = right_side - left_side
                facing = jnp.abs(diff_x + 0.9375 * diff_y + 0.75 * diff_z)
                norm = lax.rsqrt(diff_x * diff_x + diff_y * diff_y + (diff_z * diff_z + 4.0))
                lighting = facing * norm + (0.3 / 0.448)
                soft = lax.log2(1.0 + jnp.exp2(decay_slope * center + decay_offset))
                passed = transmit * jnp.exp2((center * -ray_step) * soft)
                weight = (transmit - passed) * lighting
                transmit = passed
                plain = plain + weight
                tinted = [
                    tinted[channel] + weight * jnp.tanh(slopes[channel] * center + offsets[channel]) for channel in range(3)
                ]
                previous, center = center, following
            return [0.224 * (plain + tinted[channel]) for channel in range(3)], transmit

        def chunk(half, at):
            start = pl.multiple_of(PAD + half * half_rows + at * rows_at_once, 8)
            target = pl.ds(pl.multiple_of(at * rows_at_once, 8), rows_at_once)
            colors, transmit = shaded(runs[0], start)
            if mode == "edge":
                inner = core[half, 3, target, columns]
                back_colors, back_transmit = shaded(runs[1], start)
                colors = [
                    colors[channel] + transmit * (core[half, channel, target, columns] + inner * back_colors[channel])
                    for channel in range(3)
                ]
                transmit = transmit * inner * back_transmit
            for channel in range(3):
                put(piece_at, half, channel, target, columns, colors[channel])
            put(piece_at, half, 3, target, columns, transmit)

        per_half = half_rows // rows_at_once
        if mode == "edge":
            for half in range(HALVES):
                lax.fori_loop(0, per_half, lambda at, carry, half=half: chunk(half, at) or carry, 0)
        else:
            lax.fori_loop(0, HALVES * per_half, lambda at, carry: chunk(at // per_half, lax.rem(at, per_half)) or carry, 0)

    def work():
        flag_rows = pl.ds(slots * row_cells, 8)
        flag_copies = [
            pltpu.make_async_copy(plane.at[flag_rows, :], side_flags.at[which], flag_sem.at[which])
            for which, plane in enumerate(planes)
        ]
        for copy in flag_copies:
            copy.start()
        lax.fori_loop(0, own + 2, begin_block, 0)
        for run in runs:
            for z, _ in run:
                vol[zero_slot, z, body, :] = jnp.zeros((row_cells, width), jnp.float32)
        for copy in flag_copies:
            copy.wait()
        if mode == "full":
            lax.fori_loop(0, block_count, begin_plane, (jnp.int32(0), jnp.int32(0)))
        arrive(0)
        arrive(1)
        lax.fori_loop(1, own + 1, visit, 0)

    if mode == "full":
        work()
    else:
        pl.when(ending)(work)


def shade(mode, piece_total, ray_step, flags, place, transfer, density, above, below, *others):
    depth_cells, row_cells, col_cells = density.shape
    block_count = flags.shape[0]
    width = col_cells // block_count
    own = block_count if mode == "full" else block_count // piece_total
    depth = 2 if mode == "edge" else depth_cells
    cells = own * depth * row_cells * width
    held = 6 if mode == "edge" else depth_cells + 2
    part = (4, row_cells // HALVES, col_cells // piece_total)
    pieces = {"core": (1, HALVES) + part, "edge": part, "full": (piece_total, HALVES) + part}[mode]
    out = jax.ShapeDtypeStruct(pieces, jnp.float32)
    extra = {"core": [], "edge": [VMEM, VMEM], "full": [ANY, ANY]}[mode]
    return pl.pallas_call(
        functools.partial(shade_kernel, mode, piece_total, width, ray_step),
        out_shape=(out,) * HALVES if mode == "edge" else out,
        in_specs=[SMEM] * 3 + [ANY] + [VMEM] * 2 + extra,
        out_specs=(VMEM,) * HALVES if mode == "edge" else VMEM,
        scratch_shapes=[
            pltpu.VMEM((own + 3, held, row_cells + 2 * PAD, width), jnp.float32),
            pltpu.SMEM((2, 8, width), jnp.float32),
            pltpu.SemaphoreType.DMA((2, own + 2)),
            pltpu.SemaphoreType.DMA((2, own + 2)),
            pltpu.SemaphoreType.DMA((2,)),
        ],
        compiler_params=pltpu.CompilerParams(vmem_limit_bytes=50 << 20),
        cost_estimate=pl.CostEstimate(flops=60 * cells, bytes_accessed=4 * cells, transcendentals=7 * cells),
        name=f"shade_{mode}",
    )(flags, place, transfer, density, above, below, *others)


def merge_kernel(half, table, pieces, front, back, up, down, own, sem):
    copies = [pltpu.make_async_copy(pieces.at[table[side], half], own.at[side], sem.at[side]) for side in range(2)]
    for copy in copies:
        copy.start()
    opening = jnp.where(table[2] > 0, front[3], 1.0)
    closing = jnp.where(table[3] > 0, back[3], 1.0)
    copies[0].wait()
    up[3] = opening * own[0, 3]
    for channel in range(3):
        up[channel] = front[channel] + opening * own[0, channel]
    copies[1].wait()
    passed = own[1, 3]
    down[3] = passed * closing
    for channel in range(3):
        down[channel] = own[1, channel] + passed * back[channel]


def merge(half, table, pieces, front, back):
    part = pieces.shape[2:]
    cells = part[0] * part[1] * part[2]
    return pl.pallas_call(
        functools.partial(merge_kernel, half),
        out_shape=(jax.ShapeDtypeStruct(part, jnp.float32),) * 2,
        in_specs=[SMEM, ANY, VMEM, VMEM],
        out_specs=[VMEM, VMEM],
        scratch_shapes=[pltpu.VMEM((2,) + part, jnp.float32), pltpu.SemaphoreType.DMA((2,))],
        compiler_params=pltpu.CompilerParams(vmem_limit_bytes=50 << 20),
        cost_estimate=pl.CostEstimate(flops=4 * cells, bytes_accessed=24 * cells, transcendentals=0),
        name="merge",
    )(table, pieces, front, back)


def finish_kernel(half, table, pieces, front, back, *others):
    image, own, made, sem = others[-4:]
    rows = pl.ds(half * made.shape[1], made.shape[1])
    load = pltpu.make_async_copy(pieces.at[table[0], half], own, sem.at[0])
    load.start()
    opening = jnp.where(table[2] > 0, front[3], 1.0)
    closing = jnp.where(table[3] > 0, back[3], 1.0)
    load.wait()
    passed = opening * own[3]
    for channel in range(3):
        made[channel] = front[channel] + opening * own[channel] + passed * back[channel]
    made[3] = 1.0 - passed * closing
    store = pltpu.make_async_copy(made, image.at[:, rows, :], sem.at[1])
    store.start()
    store.wait()


def finish(half, table, pieces, front, back, image):
    part = pieces.shape[2:]
    cells = part[0] * part[1] * part[2]
    started = [] if image is None else [image]
    return pl.pallas_call(
        functools.partial(finish_kernel, half),
        out_shape=jax.ShapeDtypeStruct((part[0], HALVES * part[1], part[2]), jnp.float32),
        in_specs=[SMEM, ANY, VMEM, VMEM] + [ANY] * len(started),
        out_specs=ANY,
        scratch_shapes=[pltpu.VMEM(part, jnp.float32), pltpu.VMEM(part, jnp.float32), pltpu.SemaphoreType.DMA((2,))],
        input_output_aliases={4: 0} if started else {},
        compiler_params=pltpu.CompilerParams(vmem_limit_bytes=50 << 20),
        cost_estimate=pl.CostEstimate(flops=4 * cells, bytes_accessed=16 * cells, transcendentals=0),
        name="finish",
    )(table, pieces, front, back, *started)


def shards(density, occupancy, transfer):
    depth_cells, row_cells, col_cells = density.shape
    flags = occupancy.reshape(-1)
    block_count = flags.shape[0]
    width = col_cells // block_count
    count = lax.axis_size("depth")
    slabs = lax.axis_size("rows")
    position = lax.axis_index("depth")
    ray_step = 2.0 / (depth_cells * count)
    backward = position >= count // 2
    even = lax.rem(position, 2) == 0
    ending = jnp.logical_or(position == 0, position == count - 1)
    place = jnp.stack([backward.astype(jnp.int32), even.astype(jnp.int32), ending.astype(jnp.int32)])

    def pairs(start):
        found = []
        for low in range(start, count - 1, 2):
            found += [(low, low + 1), (low + 1, low)]
        return found

    outer, inner = pack_planes(density, flags, even.astype(jnp.int32).reshape(1), width)
    outer_plane = lax.ppermute(outer, "depth", pairs(0))
    inner_plane = lax.ppermute(inner, "depth", pairs(1)) if count > 2 else jnp.zeros_like(inner)
    first_row, last_row = pack_rows(density, flags, width)
    above = lax.ppermute(last_row, "rows", [(i, i + 1) for i in range(slabs - 1)])
    below = lax.ppermute(first_row, "rows", [(i + 1, i) for i in range(slabs - 1)])
    args = (flags, place, transfer, density, above, below)
    core = shade("core", count, ray_step, *args)
    first = shade("edge", count, ray_step, *args, outer_plane, core[0])
    pieces = shade("full", count, ray_step, *args, outer_plane, inner_plane)

    def rank(piece):
        return jnp.clip(jnp.where(backward, piece, count - 1 - piece), 0, count - 1)

    def table(up_piece, down_piece):
        sides = [position > 0, position < count - 1]
        return jnp.stack([rank(up_piece), rank(down_piece)] + [side.astype(jnp.int32) for side in sides])

    fronts, backs = [None] * HALVES, [None] * HALVES
    for step in range(count - 1):
        ups = [(i, i + 1) for i in range(step + 1)]
        downs = [(count - 1 - i, count - 2 - i) for i in range(step + 1)]
        apart = step + 1 < count - 2 - step
        step_table = table(count - 1 - step + position, step + position - (count - 1))
        for half in range(HALVES):
            if step:
                up, down = merge(half, step_table, pieces, fronts[half], backs[half])
            else:
                up = down = first[half]
            if apart:
                sent = jnp.where(backward, down, up) if step else up
                fronts[half] = backs[half] = lax.ppermute(sent, "depth", ups + downs)
            else:
                fronts[half] = lax.ppermute(up, "depth", ups)
                backs[half] = lax.ppermute(down, "depth", downs)
    image = None
    final_table = table(position, position)
    for half in range(HALVES):
        image = finish(half, final_table, pieces, fronts[half], backs[half], image)
    return image


def solution(mesh):
    in_specs = (P("depth", "rows", None), P("depth", "rows", None), P())
    out_specs = P(None, "rows", "depth")
    return jax.shard_map(shards, mesh=mesh, in_specs=in_specs, out_specs=out_specs, check_vma=False)
```

```python
import functools
import jax
import jax.numpy as jnp
from jax import lax
from jax.experimental import pallas as pl
from jax.experimental.pallas import tpu as pltpu
from jax.sharding import PartitionSpec as P

OCCUPIED_MOST = 12
PAD = 8
ROWS_AT_ONCE = 32
HALVES = 2
STORES = 4
LOG2_E = 1.4426950408889634
SMEM = pl.BlockSpec(memory_space=pltpu.SMEM)
VMEM = pl.BlockSpec(memory_space=pltpu.VMEM)
ANY = pl.BlockSpec(memory_space=pl.ANY)


def pack_planes_kernel(width, flags, even, density, outer, inner, sem):
    depth_cells, row_cells, _ = density.shape
    block_count = flags.shape[0]
    slots = min(OCCUPIED_MOST, block_count)
    outer_plane = jnp.where(even[0] > 0, depth_cells - 1, 0)
    inner_plane = depth_cells - 1 - outer_plane

    def copies(block, slot):
        columns = pl.ds(pl.multiple_of(block * width, width), width)
        rows = pl.ds(pl.multiple_of(slot * row_cells, row_cells), row_cells)
        return (
            pltpu.make_async_copy(density.at[outer_plane, :, columns], outer.at[rows, :], sem.at[0, slot]),
            pltpu.make_async_copy(density.at[inner_plane, :, columns], inner.at[rows, :], sem.at[1, slot]),
        )

    def begin(block, slot):
        wanted = jnp.logical_and(flags[block] > 0, slot < slots)

        @pl.when(wanted)
        def _():
            for copy in copies(block, slot):
                copy.start()

        return slot + wanted.astype(jnp.int32)

    used = lax.fori_loop(0, block_count, begin, jnp.int32(0))
    lane = lax.broadcasted_iota(jnp.int32, (8, width), 1)
    row_of_flags = jnp.zeros((8, width), jnp.float32)
    for block in range(block_count):
        row_of_flags = jnp.where(lane == block, flags[block].astype(jnp.float32), row_of_flags)
    outer[pl.ds(slots * row_cells, 8), :] = row_of_flags
    inner[pl.ds(slots * row_cells, 8), :] = row_of_flags

    def end(slot, carry):
        for copy in copies(0, slot):
            copy.wait()
        return carry

    lax.fori_loop(0, used, end, 0)


def pack_planes(density, flags, even, width):
    row_cells = density.shape[1]
    slots = min(OCCUPIED_MOST, flags.shape[0])
    plane = jax.ShapeDtypeStruct((slots * row_cells + 8, width), jnp.float32)
    return pl.pallas_call(
        functools.partial(pack_planes_kernel, width),
        out_shape=(plane, plane),
        in_specs=[SMEM, SMEM, ANY],
        out_specs=[VMEM] * 2,
        scratch_shapes=[pltpu.SemaphoreType.DMA((2, slots))],
        compiler_params=pltpu.CompilerParams(vmem_limit_bytes=50 << 20),
        name="pack_planes",
    )(flags, even, density)


def pack_rows_kernel(width, flags, density, first_row, last_row, top, bottom, sem):
    depth_cells, row_cells, _ = density.shape
    block_count = flags.shape[0]
    top_copy = pltpu.make_async_copy(density.at[:, 0:8, :], top, sem.at[0])
    bottom_copy = pltpu.make_async_copy(density.at[:, row_cells - 8 : row_cells, :], bottom, sem.at[1])
    top_copy.start()
    bottom_copy.start()
    top_copy.wait()
    bottom_copy.wait()

    def edge(block, carry):
        columns = pl.ds(pl.multiple_of(block * width, width), width)
        flag = flags[block].astype(jnp.float32)
        for z in range(depth_cells):
            first_row[pl.ds(z, 1), columns] = top[z, 0:1, columns] * flag
            last_row[pl.ds(z, 1), columns] = bottom[z, 7:8, columns] * flag
        return carry

    lax.fori_loop(0, block_count, edge, 0)


def pack_rows(density, flags, width):
    depth_cells, _, col_cells = density.shape
    row = jax.ShapeDtypeStruct((depth_cells, col_cells), jnp.float32)
    return pl.pallas_call(
        functools.partial(pack_rows_kernel, width),
        out_shape=(row, row),
        in_specs=[SMEM, ANY],
        out_specs=[VMEM] * 2,
        scratch_shapes=[
            pltpu.VMEM((depth_cells, 8, col_cells), jnp.float32),
            pltpu.VMEM((depth_cells, 8, col_cells), jnp.float32),
            pltpu.SemaphoreType.DMA((2,)),
        ],
        compiler_params=pltpu.CompilerParams(vmem_limit_bytes=50 << 20),
        name="pack_rows",
    )(flags, density)


def shade_kernel(mode, first_at, piece_count, piece_total, width, ray_step, flags, place, transfer, density, above, below, *others):
    plane_count = {"core": 0, "edge": 1, "rim": 2, "full": 2}[mode]
    thin = mode in ("edge", "rim")
    planes = others[:plane_count]
    others = others[plane_count:]
    if thin:
        core, *others = others
    if mode == "full" and len(others) > 6:
        others = others[1:]
    *outs, vol, side_flags, block_sem, plane_sem, flag_sem = others
    depth_cells, row_cells, _ = density.shape
    block_count = flags.shape[0]
    piece_blocks = block_count // piece_total
    slots = min(OCCUPIED_MOST, block_count)
    backward = place[0] > 0
    even = place[1] > 0
    ending = place[2] > 0
    own = piece_count * piece_blocks
    zero_slot = own + 2
    first_piece = jnp.where(backward, first_at, piece_total - first_at - piece_count)
    first_block = first_piece * piece_blocks
    body = pl.ds(PAD, row_cells)
    half_rows = row_cells // HALVES
    if thin:
        held = [(1, 0, 2), (3, depth_cells - 2, 2)]
        runs = [[(1, 0)], [(4, depth_cells - 1)]]
        low_at, high_at = 0, 5
    else:
        held = [(1, 0, depth_cells)]
        trim = 1 if mode == "core" else 0
        runs = [[(z + 1, z) for z in range(trim, depth_cells - trim)]]
        low_at, high_at = 0, depth_cells + 1

    def put(piece_at, half, channel, rows, columns, value):
        if mode == "edge":
            outs[half][channel, rows, columns] = value
        else:
            outs[0][piece_at, half, channel, rows, columns] = value

    def block_of(slot):
        return first_block + slot - 1

    def occupied(block):
        inside = jnp.logical_and(block >= 0, block < block_count)
        return jnp.logical_and(inside, flags[jnp.clip(block, 0, block_count - 1)] > 0)

    def block_copies(slot):
        block = jnp.clip(block_of(slot), 0, block_count - 1)
        columns = pl.ds(pl.multiple_of(block * width, width), width)
        return [
            pltpu.make_async_copy(
                density.at[pl.ds(z, count), :, columns], vol.at[slot, pl.ds(at, count), body, :], block_sem.at[part, slot]
            )
            for part, (at, z, count) in enumerate(held)
        ]

    def plane_copy(side, which, slot, rank):
        rows = pl.ds(pl.multiple_of(rank * row_cells, row_cells), row_cells)
        at = high_at if side else low_at
        return pltpu.make_async_copy(planes[which].at[rows, :], vol.at[slot, at, body, :], plane_sem.at[side, slot])

    def near(side, block):
        if mode == "edge":
            return jnp.logical_and(backward if side == 0 else jnp.logical_not(backward), side_flags[0, 0, block] > 0.5)
        which = jnp.where(even, 1 - side, side)
        return side_flags[which, 0, block] > 0.5

    def begin_block(slot, carry):
        @pl.when(occupied(block_of(slot)))
        def _():
            for copy in block_copies(slot):
                copy.start()

        return carry

    def begin_plane(block, ranks):
        slot = block - first_block + 1
        mine = jnp.logical_and(jnp.logical_and(slot >= 1, slot <= own), flags[block] > 0)
        after_this = []
        for side in range(2):
            close = near(side, block)
            wanted = jnp.logical_and(mine, close)
            for which in range(2):
                chosen = even if which != side else jnp.logical_not(even)

                @pl.when(jnp.logical_and(wanted, chosen))
                def _():
                    plane_copy(side, which, slot, ranks[side]).start()

            after_this.append(ranks[side] + close.astype(jnp.int32))
        return tuple(after_this)

    def arrive(slot):
        @pl.when(occupied(block_of(slot)))
        def _():
            for copy in block_copies(slot):
                copy.wait()

    def visit(slot, carry):
        block = block_of(slot)
        piece = block // piece_blocks - first_piece
        at = jnp.where(backward, piece, piece_count - 1 - piece)
        columns = pl.ds(pl.multiple_of(lax.rem(block, piece_blocks) * width, width), width)
        arrive(slot + 1)

        @pl.when(jnp.logical_not(occupied(block)))
        def _():
            for half in range(HALVES):
                for channel in range(4):
                    value = 1.0 if channel == 3 else 0.0
                    put(at, half, channel, slice(None), columns, jnp.full((half_rows, width), value, jnp.float32))

        @pl.when(occupied(block))
        def _():
            left = jnp.where(occupied(block - 1), slot - 1, zero_slot)
            right = jnp.where(occupied(block + 1), slot + 1, zero_slot)
            source = pl.ds(pl.multiple_of(block * width, width), width)
            for run in runs:
                for z, depth in run:
                    vol[slot, z, pl.ds(PAD - 1, 1), :] = above[pl.ds(depth, 1), source]
                    vol[slot, z, pl.ds(PAD + row_cells, 1), :] = below[pl.ds(depth, 1), source]
            for side in range(2 if planes else 0):
                close = near(side, block)
                side_at = high_at if side else low_at

                if mode == "full":

                    @pl.when(close)
                    def _():
                        plane_copy(side, 0, slot, 0).wait()

                else:
                    for which in range(plane_count):
                        chosen = True if plane_count == 1 else (even if which != side else jnp.logical_not(even))

                        @pl.when(jnp.logical_and(close, chosen))
                        def _():
                            rank = lax.fori_loop(
                                0, block, lambda i, found: found + jnp.where(side_flags[which, 0, i] > 0.5, 1, 0), jnp.int32(0)
                            )
                            rows = pl.ds(pl.multiple_of(rank * row_cells, row_cells), row_cells)
                            vol[slot, side_at, body, :] = planes[which][rows, :]

                @pl.when(jnp.logical_not(close))
                def _():
                    vol[slot, side_at, body, :] = jnp.zeros((row_cells, width), jnp.float32)

            march(slot, left, right, at, columns)

        return carry

    def march(slot, left, right, piece_at, columns):
        rows_at_once = half_rows if thin else min(ROWS_AT_ONCE, half_rows)
        shape = (rows_at_once, width)
        lane = lax.broadcasted_iota(jnp.int32, shape, 1)
        at_first = lane == 0
        at_last = lane == width - 1
        slopes = [transfer[0, channel] * 0.5 for channel in range(3)]
        offsets = [transfer[1, channel] * 0.5 for channel in range(3)]
        decay_slope = transfer[0, 3] * LOG2_E
        decay_offset = transfer[1, 3] * LOG2_E

        def shaded(run, start):
            rows = pl.ds(start, rows_at_once)
            previous = vol[slot, run[0][0] - 1, rows, :]
            center = vol[slot, run[0][0], rows, :]
            transmit = jnp.ones(shape, jnp.float32)
            plain = jnp.zeros(shape, jnp.float32)
            tinted = [plain] * 3
            for z, _ in run:
                following = vol[slot, z + 1, rows, :]
                diff_z = following - previous
                diff_y = vol[slot, z, pl.ds(start + 1, rows_at_once), :] - vol[slot, z, pl.ds(start - 1, rows_at_once), :]
                right_side = pltpu.roll(jnp.where(at_first, vol[right, z, rows, :], center), width - 1, 1)
                left_side = pltpu.roll(jnp.where(at_last, vol[left, z, rows, :], center), 1, 1)
                diff_x = right_side - left_side
                facing = jnp.abs(diff_x + 0.9375 * diff_y + 0.75 * diff_z)
                norm = lax.rsqrt(diff_x * diff_x + diff_y * diff_y + (diff_z * diff_z + 4.0))
                lighting = facing * norm + (0.3 / 0.448)
                soft = lax.log2(1.0 + jnp.exp2(decay_slope * center + decay_offset))
                passed = transmit * jnp.exp2((center * -ray_step) * soft)
                weight = (transmit - passed) * lighting
                transmit = passed
                plain = plain + weight
                tinted = [
                    tinted[channel] + weight * jnp.tanh(slopes[channel] * center + offsets[channel]) for channel in range(3)
                ]
                previous, center = center, following
            return [0.224 * (plain + tinted[channel]) for channel in range(3)], transmit

        def chunk(half, at):
            start = pl.multiple_of(PAD + half * half_rows + at * rows_at_once, 8)
            target = pl.ds(pl.multiple_of(at * rows_at_once, 8), rows_at_once)
            colors, transmit = shaded(runs[0], start)
            if thin:
                inner = core[half, 3, target, columns]
                back_colors, back_transmit = shaded(runs[1], start)
                colors = [
                    colors[channel] + transmit * (core[half, channel, target, columns] + inner * back_colors[channel])
                    for channel in range(3)
                ]
                transmit = transmit * inner * back_transmit
            for channel in range(3):
                put(piece_at, half, channel, target, columns, colors[channel])
            put(piece_at, half, 3, target, columns, transmit)

        per_half = half_rows // rows_at_once
        if mode == "edge":
            for half in range(HALVES):
                chunk(half, 0)
        else:
            lax.fori_loop(0, HALVES * per_half, lambda at, carry: chunk(at // per_half, lax.rem(at, per_half)) or carry, 0)

    def work():
        flag_rows = pl.ds(slots * row_cells, 8)
        flag_copies = [
            pltpu.make_async_copy(plane.at[flag_rows, :], side_flags.at[which], flag_sem.at[which])
            for which, plane in enumerate(planes)
        ]
        for copy in flag_copies:
            copy.start()
        lax.fori_loop(0, own + 2, begin_block, 0)
        for run in runs:
            for z, _ in run:
                vol[zero_slot, z, body, :] = jnp.zeros((row_cells, width), jnp.float32)
        for copy in flag_copies:
            copy.wait()
        if mode == "full":
            lax.fori_loop(0, block_count, begin_plane, (jnp.int32(0), jnp.int32(0)))
        arrive(0)
        arrive(1)
        lax.fori_loop(1, own + 1, visit, 0)

    if thin:
        pl.when(ending if mode == "edge" else jnp.logical_not(ending))(work)
    else:
        work()


def shade(mode, first_at, piece_count, piece_total, ray_step, flags, place, transfer, density, above, below, *others):
    depth_cells, row_cells, col_cells = density.shape
    block_count = flags.shape[0]
    width = col_cells // block_count
    own = piece_count * (block_count // piece_total)
    thin = mode in ("edge", "rim")
    depth = 2 if thin else depth_cells
    cells = own * depth * row_cells * width
    held = 6 if thin else depth_cells + 2
    part = (4, row_cells // HALVES, col_cells // piece_total)
    out = jax.ShapeDtypeStruct(part if mode == "edge" else (piece_count, HALVES) + part, jnp.float32)
    extra = {"core": [], "edge": [VMEM] * 2, "rim": [VMEM] * 3, "full": [ANY] * 2}[mode]
    extra = extra + [SMEM] * (len(others) - len(extra))
    return pl.pallas_call(
        functools.partial(shade_kernel, mode, first_at, piece_count, piece_total, width, ray_step),
        out_shape=(out,) * HALVES if mode == "edge" else out,
        in_specs=[SMEM] * 3 + [ANY] + [VMEM] * 2 + extra,
        out_specs=(VMEM,) * HALVES if mode == "edge" else VMEM,
        scratch_shapes=[
            pltpu.VMEM((own + 3, held, row_cells + 2 * PAD, width), jnp.float32),
            pltpu.SMEM((2, 8, width), jnp.float32),
            pltpu.SemaphoreType.DMA((2, own + 2)),
            pltpu.SemaphoreType.DMA((2, own + 2)),
            pltpu.SemaphoreType.DMA((2,)),
        ],
        compiler_params=pltpu.CompilerParams(vmem_limit_bytes=50 << 20),
        cost_estimate=pl.CostEstimate(flops=60 * cells, bytes_accessed=4 * cells, transcendentals=7 * cells),
        name=f"shade_{mode}_{first_at}",
    )(flags, place, transfer, density, above, below, *others)


def fetch(half, at, pieces, own, sem):
    at = jnp.minimum(at, sum(piece.shape[0] for piece in pieces) - 1)
    first = 0
    for piece in pieces:
        here = jnp.logical_and(at >= first, at < first + piece.shape[0])

        @pl.when(here)
        def _():
            pltpu.make_async_copy(piece.at[at - first, half], own, sem).start()

        first += piece.shape[0]
    return pltpu.make_async_copy(pieces[0].at[0, 0], own, sem)


def merge_kernel(half, table, front, back, *others):
    *pieces, up, down, token, own, sem = others
    copies = [fetch(half, table[side], pieces, own.at[side], sem.at[side]) for side in range(2)]
    token[0] = table[0]
    opening = jnp.where(table[2] > 0, front[3], 1.0)
    closing = jnp.where(table[3] > 0, back[3], 1.0)
    copies[0].wait()
    up[3] = opening * own[0, 3]
    for channel in range(3):
        up[channel] = front[channel] + opening * own[0, channel]
    copies[1].wait()
    passed = own[1, 3]
    down[3] = passed * closing
    for channel in range(3):
        down[channel] = own[1, channel] + passed * back[channel]


def merge(half, table, pieces, front, back):
    part = pieces[0].shape[2:]
    cells = part[0] * part[1] * part[2]
    return pl.pallas_call(
        functools.partial(merge_kernel, half),
        out_shape=(jax.ShapeDtypeStruct(part, jnp.float32),) * 2 + (jax.ShapeDtypeStruct((1,), jnp.int32),),
        in_specs=[SMEM, VMEM, VMEM] + [ANY] * len(pieces),
        out_specs=[VMEM, VMEM, SMEM],
        scratch_shapes=[pltpu.VMEM((2,) + part, jnp.float32), pltpu.SemaphoreType.DMA((2,))],
        compiler_params=pltpu.CompilerParams(vmem_limit_bytes=50 << 20),
        cost_estimate=pl.CostEstimate(flops=4 * cells, bytes_accessed=24 * cells, transcendentals=0),
        name="merge",
    )(table, front, back, *pieces)


def finish_kernel(half, table, front, back, *others):
    *pieces, image, own, made, load_sem, store_sem = others
    if half:
        pieces = pieces[:-1]
    load = fetch(half, table[0], pieces, own, load_sem)
    part_rows = made.shape[1] // STORES
    stores = []
    load.wait()
    for at in range(STORES):
        rows = pl.ds(at * part_rows, part_rows)
        target = pl.ds(half * made.shape[1] + at * part_rows, part_rows)
        opening = jnp.where(table[2] > 0, front[3, rows], 1.0)
        closing = jnp.where(table[3] > 0, back[3, rows], 1.0)
        passed = opening * own[3, rows]
        for channel in range(3):
            made[channel, rows] = front[channel, rows] + opening * own[channel, rows] + passed * back[channel, rows]
        made[3, rows] = 1.0 - passed * closing
        stores.append(pltpu.make_async_copy(made.at[:, rows, :], image.at[:, target, :], store_sem.at[at]))
        stores[-1].start()
    for store in stores:
        store.wait()


def finish(half, table, pieces, front, back, image):
    part = pieces[0].shape[2:]
    cells = part[0] * part[1] * part[2]
    started = [] if image is None else [image]
    return pl.pallas_call(
        functools.partial(finish_kernel, half),
        out_shape=jax.ShapeDtypeStruct((part[0], HALVES * part[1], part[2]), jnp.float32),
        in_specs=[SMEM, VMEM, VMEM] + [ANY] * (len(pieces) + len(started)),
        out_specs=ANY,
        scratch_shapes=[
            pltpu.VMEM(part, jnp.float32),
            pltpu.VMEM(part, jnp.float32),
            pltpu.SemaphoreType.DMA,
            pltpu.SemaphoreType.DMA((STORES,)),
        ],
        input_output_aliases={3 + len(pieces): 0} if started else {},
        compiler_params=pltpu.CompilerParams(vmem_limit_bytes=50 << 20),
        cost_estimate=pl.CostEstimate(flops=4 * cells, bytes_accessed=16 * cells, transcendentals=0),
        name="finish",
    )(table, front, back, *pieces, *started)


def shards(density, occupancy, transfer):
    depth_cells, row_cells, col_cells = density.shape
    flags = occupancy.reshape(-1)
    block_count = flags.shape[0]
    width = col_cells // block_count
    count = lax.axis_size("depth")
    slabs = lax.axis_size("rows")
    position = lax.axis_index("depth")
    ray_step = 2.0 / (depth_cells * count)
    backward = position >= count // 2
    even = lax.rem(position, 2) == 0
    ending = jnp.logical_or(position == 0, position == count - 1)
    place = jnp.stack([backward.astype(jnp.int32), even.astype(jnp.int32), ending.astype(jnp.int32)])

    def pairs(start):
        found = []
        for low in range(start, count - 1, 2):
            found += [(low, low + 1), (low + 1, low)]
        return found

    outer, inner = pack_planes(density, flags, even.astype(jnp.int32).reshape(1), width)
    outer_plane = lax.ppermute(outer, "depth", pairs(0))
    inner_plane = lax.ppermute(inner, "depth", pairs(1)) if count > 2 else jnp.zeros_like(inner)
    first_row, last_row = pack_rows(density, flags, width)
    above = lax.ppermute(last_row, "rows", [(i, i + 1) for i in range(slabs - 1)])
    below = lax.ppermute(first_row, "rows", [(i + 1, i) for i in range(slabs - 1)])
    args = (flags, place, transfer, density, above, below)
    ahead = count // 2
    core = shade("core", 0, 1, count, ray_step, *args)
    first = shade("edge", 0, 1, count, ray_step, *args, outer_plane, core[0])
    pieces = [
        shade("rim", 0, 1, count, ray_step, *args, outer_plane, inner_plane, core[0]),
        shade("full", 1, ahead, count, ray_step, *args, outer_plane, inner_plane),
    ]

    def rank(piece):
        return jnp.clip(jnp.where(backward, piece, count - 1 - piece), 0, count - 1)

    def table(up_piece, down_piece):
        sides = [position > 0, position < count - 1]
        return jnp.stack([rank(up_piece), rank(down_piece)] + [side.astype(jnp.int32) for side in sides])

    fronts, backs = [None] * HALVES, [None] * HALVES
    token = None
    for step in range(count - 1):
        ups = [(i, i + 1) for i in range(step + 1)]
        downs = [(count - 1 - i, count - 2 - i) for i in range(step + 1)]
        apart = step + 1 < count - 2 - step
        step_table = table(count - 1 - step + position, step + position - (count - 1))
        if step == ahead:
            pieces.append(shade("full", 1 + ahead, count - 1 - ahead, count, ray_step, *args, outer_plane, inner_plane, token))
        for half in range(HALVES):
            if step:
                up, down, token = merge(half, step_table, pieces, fronts[half], backs[half])
            else:
                up = down = first[half]
            if apart:
                sent = jnp.where(backward, down, up) if step else up
                fronts[half] = backs[half] = lax.ppermute(sent, "depth", ups + downs)
            else:
                fronts[half] = lax.ppermute(up, "depth", ups)
                backs[half] = lax.ppermute(down, "depth", downs)
    image = None
    final_table = table(position, position)
    for half in range(HALVES):
        image = finish(half, final_table, pieces, fronts[half], backs[half], image)
    return image


def solution(mesh):
    in_specs = (P("depth", "rows", None), P("depth", "rows", None), P())
    out_specs = P(None, "rows", "depth")
    return jax.shard_map(shards, mesh=mesh, in_specs=in_specs, out_specs=out_specs, check_vma=False)
```

```python
import functools
import jax
import jax.numpy as jnp
from jax import lax
from jax.experimental import pallas as pl
from jax.experimental.pallas import tpu as pltpu
from jax.sharding import PartitionSpec as P

OCCUPIED_MOST = 12
PAD = 8
ROWS_AT_ONCE = 32
HALVES = 2
CHUNKS = 4
LOG2_E = 1.4426950408889634
SMEM = pl.BlockSpec(memory_space=pltpu.SMEM)
VMEM = pl.BlockSpec(memory_space=pltpu.VMEM)
ANY = pl.BlockSpec(memory_space=pl.ANY)


def pack_planes_kernel(width, flags, even, density, outer, inner, sem):
    depth_cells, row_cells, _ = density.shape
    block_count = flags.shape[0]
    slots = min(OCCUPIED_MOST, block_count)
    outer_plane = jnp.where(even[0] > 0, depth_cells - 1, 0)
    inner_plane = depth_cells - 1 - outer_plane

    def copies(block, slot):
        columns = pl.ds(pl.multiple_of(block * width, width), width)
        rows = pl.ds(pl.multiple_of(slot * row_cells, row_cells), row_cells)
        return (
            pltpu.make_async_copy(density.at[outer_plane, :, columns], outer.at[rows, :], sem.at[0, slot]),
            pltpu.make_async_copy(density.at[inner_plane, :, columns], inner.at[rows, :], sem.at[1, slot]),
        )

    def begin(block, slot):
        wanted = jnp.logical_and(flags[block] > 0, slot < slots)

        @pl.when(wanted)
        def _():
            for copy in copies(block, slot):
                copy.start()

        return slot + wanted.astype(jnp.int32)

    used = lax.fori_loop(0, block_count, begin, jnp.int32(0))
    lane = lax.broadcasted_iota(jnp.int32, (8, width), 1)
    row_of_flags = jnp.zeros((8, width), jnp.float32)
    for block in range(block_count):
        row_of_flags = jnp.where(lane == block, flags[block].astype(jnp.float32), row_of_flags)
    outer[pl.ds(slots * row_cells, 8), :] = row_of_flags
    inner[pl.ds(slots * row_cells, 8), :] = row_of_flags

    def end(slot, carry):
        for copy in copies(0, slot):
            copy.wait()
        return carry

    lax.fori_loop(0, used, end, 0)


def pack_planes(density, flags, even, width):
    row_cells = density.shape[1]
    slots = min(OCCUPIED_MOST, flags.shape[0])
    plane = jax.ShapeDtypeStruct((slots * row_cells + 8, width), jnp.float32)
    return pl.pallas_call(
        functools.partial(pack_planes_kernel, width),
        out_shape=(plane, plane),
        in_specs=[SMEM, SMEM, ANY],
        out_specs=[VMEM] * 2,
        scratch_shapes=[pltpu.SemaphoreType.DMA((2, slots))],
        compiler_params=pltpu.CompilerParams(vmem_limit_bytes=50 << 20),
        name="pack_planes",
    )(flags, even, density)


def pack_rows_kernel(width, flags, density, first_row, last_row, top, bottom, sem):
    depth_cells, row_cells, _ = density.shape
    block_count = flags.shape[0]
    top_copy = pltpu.make_async_copy(density.at[:, 0:8, :], top, sem.at[0])
    bottom_copy = pltpu.make_async_copy(density.at[:, row_cells - 8 : row_cells, :], bottom, sem.at[1])
    top_copy.start()
    bottom_copy.start()
    top_copy.wait()
    bottom_copy.wait()

    def edge(block, carry):
        columns = pl.ds(pl.multiple_of(block * width, width), width)
        flag = flags[block].astype(jnp.float32)
        for z in range(depth_cells):
            first_row[pl.ds(z, 1), columns] = top[z, 0:1, columns] * flag
            last_row[pl.ds(z, 1), columns] = bottom[z, 7:8, columns] * flag
        return carry

    lax.fori_loop(0, block_count, edge, 0)


def pack_rows(density, flags, width):
    depth_cells, _, col_cells = density.shape
    row = jax.ShapeDtypeStruct((depth_cells, col_cells), jnp.float32)
    return pl.pallas_call(
        functools.partial(pack_rows_kernel, width),
        out_shape=(row, row),
        in_specs=[SMEM, ANY],
        out_specs=[VMEM] * 2,
        scratch_shapes=[
            pltpu.VMEM((depth_cells, 8, col_cells), jnp.float32),
            pltpu.VMEM((depth_cells, 8, col_cells), jnp.float32),
            pltpu.SemaphoreType.DMA((2,)),
        ],
        compiler_params=pltpu.CompilerParams(vmem_limit_bytes=50 << 20),
        name="pack_rows",
    )(flags, density)


def shade_kernel(mode, first_at, piece_count, piece_total, width, ray_step, flags, place, transfer, density, above, below, *others):
    plane_count = {"core": 0, "edge": 1, "rim": 2, "full": 2}[mode]
    thin = mode in ("edge", "rim")
    planes = others[:plane_count]
    others = others[plane_count:]
    if thin:
        core, others = others[:HALVES], others[HALVES:]
    *others, token, vol, side_flags, block_sem, plane_sem, flag_sem = others
    outs = others[-HALVES * piece_count :]
    token[0] = flags[0]
    depth_cells, row_cells, _ = density.shape
    block_count = flags.shape[0]
    piece_blocks = block_count // piece_total
    slots = min(OCCUPIED_MOST, block_count)
    backward = place[0] > 0
    even = place[1] > 0
    ending = place[2] > 0
    own = piece_count * piece_blocks
    zero_slot = own + 2
    first_piece = jnp.where(backward, first_at, piece_total - first_at - piece_count)
    first_block = first_piece * piece_blocks
    body = pl.ds(PAD, row_cells)
    half_rows = row_cells // HALVES
    if thin:
        held = [(1, 0, 2), (3, depth_cells - 2, 2)]
        runs = [[(1, 0)], [(4, depth_cells - 1)]]
        low_at, high_at = 0, 5
    else:
        held = [(1, 0, depth_cells)]
        trim = 1 if mode == "core" else 0
        runs = [[(z + 1, z) for z in range(trim, depth_cells - trim)]]
        low_at, high_at = 0, depth_cells + 1

    def put(piece_at, half, rows, columns, values):
        for at in range(piece_count):
            for part in range(HALVES):

                @pl.when(jnp.logical_and(piece_at == at, half == part))
                def _():
                    for channel in range(4):
                        outs[at * HALVES + part][channel, rows, columns] = values[channel]

    def block_of(slot):
        return first_block + slot - 1

    def occupied(block):
        inside = jnp.logical_and(block >= 0, block < block_count)
        return jnp.logical_and(inside, flags[jnp.clip(block, 0, block_count - 1)] > 0)

    def block_copies(slot):
        block = jnp.clip(block_of(slot), 0, block_count - 1)
        columns = pl.ds(pl.multiple_of(block * width, width), width)
        return [
            pltpu.make_async_copy(
                density.at[pl.ds(z, count), :, columns], vol.at[slot, pl.ds(at, count), body, :], block_sem.at[part, slot]
            )
            for part, (at, z, count) in enumerate(held)
        ]

    def plane_copy(side, which, slot, rank):
        rows = pl.ds(pl.multiple_of(rank * row_cells, row_cells), row_cells)
        at = high_at if side else low_at
        return pltpu.make_async_copy(planes[which].at[rows, :], vol.at[slot, at, body, :], plane_sem.at[side, slot])

    def near(side, block):
        if mode == "edge":
            return jnp.logical_and(backward if side == 0 else jnp.logical_not(backward), side_flags[0, 0, block] > 0.5)
        which = jnp.where(even, 1 - side, side)
        return side_flags[which, 0, block] > 0.5

    def begin_block(slot, carry):
        @pl.when(occupied(block_of(slot)))
        def _():
            for copy in block_copies(slot):
                copy.start()

        return carry

    def begin_plane(block, ranks):
        slot = block - first_block + 1
        mine = jnp.logical_and(jnp.logical_and(slot >= 1, slot <= own), flags[block] > 0)
        after_this = []
        for side in range(2):
            close = near(side, block)
            wanted = jnp.logical_and(mine, close)
            for which in range(2):
                chosen = even if which != side else jnp.logical_not(even)

                @pl.when(jnp.logical_and(wanted, chosen))
                def _():
                    plane_copy(side, which, slot, ranks[side]).start()

            after_this.append(ranks[side] + close.astype(jnp.int32))
        return tuple(after_this)

    def arrive(slot):
        @pl.when(occupied(block_of(slot)))
        def _():
            for copy in block_copies(slot):
                copy.wait()

    def later_ranks(block, ranks):
        return tuple(rank + jnp.where(side_flags[which, 0, block] > 0.5, 1, 0) for which, rank in enumerate(ranks))

    def visit(slot, carry):
        block = block_of(slot)
        piece = block // piece_blocks - first_piece
        at = jnp.where(backward, piece, piece_count - 1 - piece)
        columns = pl.ds(pl.multiple_of(lax.rem(block, piece_blocks) * width, width), width)
        arrive(slot + 1)

        @pl.when(jnp.logical_not(occupied(block)))
        def _():
            blank = jnp.zeros((half_rows, width), jnp.float32)
            for half in range(HALVES):
                put(at, half, slice(None), columns, [blank, blank, blank, blank + 1.0])

        @pl.when(occupied(block))
        def _():
            left = jnp.where(occupied(block - 1), slot - 1, zero_slot)
            right = jnp.where(occupied(block + 1), slot + 1, zero_slot)
            source = pl.ds(pl.multiple_of(block * width, width), width)
            for run in runs:
                for z, depth in run:
                    vol[slot, z, pl.ds(PAD - 1, 1), :] = above[pl.ds(depth, 1), source]
                    vol[slot, z, pl.ds(PAD + row_cells, 1), :] = below[pl.ds(depth, 1), source]
            for side in range(2 if planes else 0):
                close = near(side, block)
                side_at = high_at if side else low_at

                if mode == "full":

                    @pl.when(close)
                    def _():
                        plane_copy(side, 0, slot, 0).wait()

                else:
                    for which in range(plane_count):
                        chosen = True if plane_count == 1 else (even if which != side else jnp.logical_not(even))

                        @pl.when(jnp.logical_and(close, chosen))
                        def _():
                            rows = pl.ds(pl.multiple_of(carry[which] * row_cells, row_cells), row_cells)
                            vol[slot, side_at, body, :] = planes[which][rows, :]

                @pl.when(jnp.logical_not(close))
                def _():
                    vol[slot, side_at, body, :] = jnp.zeros((row_cells, width), jnp.float32)

            march(slot, left, right, at, columns)

        return carry if not thin else later_ranks(block, carry)

    def march(slot, left, right, piece_at, columns):
        rows_at_once = half_rows if thin else min(ROWS_AT_ONCE, half_rows)
        shape = (rows_at_once, width)
        lane = lax.broadcasted_iota(jnp.int32, shape, 1)
        at_first = lane == 0
        at_last = lane == width - 1
        slopes = [transfer[0, channel] * 0.5 for channel in range(3)]
        offsets = [transfer[1, channel] * 0.5 for channel in range(3)]
        decay_slope = transfer[0, 3] * LOG2_E
        decay_offset = transfer[1, 3] * LOG2_E

        def shaded(run, start):
            rows = pl.ds(start, rows_at_once)
            previous = vol[slot, run[0][0] - 1, rows, :]
            center = vol[slot, run[0][0], rows, :]
            transmit = jnp.ones(shape, jnp.float32)
            plain = jnp.zeros(shape, jnp.float32)
            tinted = [plain] * 3
            for z, _ in run:
                following = vol[slot, z + 1, rows, :]
                diff_z = following - previous
                diff_y = vol[slot, z, pl.ds(start + 1, rows_at_once), :] - vol[slot, z, pl.ds(start - 1, rows_at_once), :]
                right_side = pltpu.roll(jnp.where(at_first, vol[right, z, rows, :], center), width - 1, 1)
                left_side = pltpu.roll(jnp.where(at_last, vol[left, z, rows, :], center), 1, 1)
                diff_x = right_side - left_side
                facing = jnp.abs(diff_x + 0.9375 * diff_y + 0.75 * diff_z)
                norm = lax.rsqrt(diff_x * diff_x + diff_y * diff_y + (diff_z * diff_z + 4.0))
                lighting = facing * norm + (0.3 / 0.448)
                soft = lax.log2(1.0 + jnp.exp2(decay_slope * center + decay_offset))
                passed = transmit * jnp.exp2((center * -ray_step) * soft)
                weight = (transmit - passed) * lighting
                transmit = passed
                plain = plain + weight
                tinted = [
                    tinted[channel] + weight * jnp.tanh(slopes[channel] * center + offsets[channel]) for channel in range(3)
                ]
                previous, center = center, following
            return [0.224 * (plain + tinted[channel]) for channel in range(3)], transmit

        def chunk(half, at):
            start = pl.multiple_of(PAD + half * half_rows + at * rows_at_once, 8)
            target = pl.ds(pl.multiple_of(at * rows_at_once, 8), rows_at_once)
            colors, transmit = shaded(runs[0], start)
            if thin:
                inner = core[half][3, target, columns]
                back_colors, back_transmit = shaded(runs[1], start)
                colors = [
                    colors[channel] + transmit * (core[half][channel, target, columns] + inner * back_colors[channel])
                    for channel in range(3)
                ]
                transmit = transmit * inner * back_transmit
            put(piece_at, half, target, columns, colors + [transmit])

        per_half = half_rows // rows_at_once
        if thin:
            for half in range(HALVES):
                chunk(half, 0)
        else:
            lax.fori_loop(0, HALVES * per_half, lambda at, carry: chunk(at // per_half, lax.rem(at, per_half)) or carry, 0)

    def work():
        flag_rows = pl.ds(slots * row_cells, 8)
        flag_copies = [
            pltpu.make_async_copy(plane.at[flag_rows, :], side_flags.at[which], flag_sem.at[which])
            for which, plane in enumerate(planes)
        ]
        for copy in flag_copies:
            copy.start()
        lax.fori_loop(0, own + 2, begin_block, 0)
        for run in runs:
            for z, _ in run:
                vol[zero_slot, z, body, :] = jnp.zeros((row_cells, width), jnp.float32)
        for copy in flag_copies:
            copy.wait()
        if mode == "full":
            lax.fori_loop(0, block_count, begin_plane, (jnp.int32(0), jnp.int32(0)))
        arrive(0)
        arrive(1)
        ranks = lax.fori_loop(0, first_block, later_ranks, (jnp.int32(0),) * plane_count) if thin else 0
        lax.fori_loop(1, own + 1, visit, ranks)

    if thin:
        pl.when(ending if mode == "edge" else jnp.logical_not(ending))(work)
    else:
        work()


def shade(mode, first_at, piece_count, piece_total, ray_step, flags, place, transfer, density, above, below, *others):
    depth_cells, row_cells, col_cells = density.shape
    block_count = flags.shape[0]
    width = col_cells // block_count
    own = piece_count * (block_count // piece_total)
    thin = mode in ("edge", "rim")
    depth = 2 if thin else depth_cells
    cells = own * depth * row_cells * width
    held = 6 if thin else depth_cells + 2
    part = (4, row_cells // HALVES, col_cells // piece_total)
    out = jax.ShapeDtypeStruct(part, jnp.float32)
    outs = HALVES * piece_count
    extra = {"core": [], "edge": [VMEM] * (1 + HALVES), "rim": [VMEM] * (2 + HALVES), "full": [ANY] * 2}[mode]
    extra = extra + [SMEM] * (len(others) - len(extra))
    return pl.pallas_call(
        functools.partial(shade_kernel, mode, first_at, piece_count, piece_total, width, ray_step),
        out_shape=(out,) * outs + (jax.ShapeDtypeStruct((1,), jnp.int32),),
        in_specs=[SMEM] * 3 + [ANY] + [VMEM] * 2 + extra,
        out_specs=(VMEM,) * outs + (SMEM,),
        scratch_shapes=[
            pltpu.VMEM((own + 3, held, row_cells + 2 * PAD, width), jnp.float32),
            pltpu.SMEM((2, 8, width), jnp.float32),
            pltpu.SemaphoreType.DMA((2, own + 2)),
            pltpu.SemaphoreType.DMA((2, own + 2)),
            pltpu.SemaphoreType.DMA((2,)),
        ],
        compiler_params=pltpu.CompilerParams(vmem_limit_bytes=50 << 20),
        cost_estimate=pl.CostEstimate(flops=60 * cells, bytes_accessed=4 * cells, transcendentals=7 * cells),
        name=f"shade_{mode}_{first_at}",
    )(flags, place, transfer, density, above, below, *others)


def load_chosen(chosen, sources, buffer, sem):
    step = buffer.shape[1] // CHUNKS
    for at, source in enumerate(sources):

        @pl.when(chosen == at)
        def _():
            for chunk in range(CHUNKS):
                rows = pl.ds(chunk * step, step)
                pltpu.make_async_copy(source.at[:, rows, :], buffer.at[:, rows, :], sem.at[chunk]).start()

    def wait(chunk):
        rows = pl.ds(chunk * step, step)
        pltpu.make_async_copy(sources[0].at[:, rows, :], buffer.at[:, rows, :], sem.at[chunk]).wait()

    return wait


def compose_kernel(base, own_count, config, *others):
    *sources, _, out, token, own, got, made, own_sem, got_sem, made_sem = others
    step = own.shape[1] // CHUNKS
    token[0] = config[0]

    @pl.when(config[base] > 0)
    def _():
        own_wait = load_chosen(config[base + 1], sources[:own_count], own, own_sem)
        got_wait = load_chosen(config[base + 2], sources[own_count:], got, got_sem)
        stores = []
        for chunk in range(CHUNKS):
            rows = pl.ds(chunk * step, step)
            own_wait(chunk)
            got_wait(chunk)
            for upward, front, back in ((True, got, own), (False, own, got)):

                @pl.when((config[base + 3] > 0) == upward)
                def _():
                    passed = front[3, rows]
                    for channel in range(3):
                        made[channel, rows] = front[channel, rows] + passed * back[channel, rows]
                    made[3, rows] = passed * back[3, rows]

            stores.append(pltpu.make_async_copy(made.at[:, rows, :], out.at[:, rows, :], made_sem.at[chunk]))
            stores[-1].start()
        for store in stores:
            store.wait()


def compose(base, config, owns, gots, after):
    part = owns[0].shape
    cells = part[0] * part[1] * part[2]
    return pl.pallas_call(
        functools.partial(compose_kernel, base, len(owns)),
        out_shape=(jax.ShapeDtypeStruct(part, jnp.float32), jax.ShapeDtypeStruct((1,), jnp.int32)),
        in_specs=[SMEM] + [ANY] * (len(owns) + len(gots)) + [SMEM],
        out_specs=(ANY, SMEM),
        scratch_shapes=[pltpu.VMEM(part, jnp.float32)] * 3 + [pltpu.SemaphoreType.DMA((CHUNKS,))] * 3,
        compiler_params=pltpu.CompilerParams(vmem_limit_bytes=50 << 20),
        cost_estimate=pl.CostEstimate(flops=2 * cells, bytes_accessed=12 * cells, transcendentals=0),
        name="compose",
    )(config, *owns, *gots, after)


def finish_kernel(base, half, own_count, config, *others):
    *sources, image, own, front, back, made, own_sem, front_sem, back_sem, made_sem = others
    if half:
        sources = sources[:-1]
    has_front, has_back = config[base + 1] >= 0, config[base + 2] >= 0
    own_wait = load_chosen(config[base], sources[:own_count], own, own_sem)
    front_wait = load_chosen(config[base + 1], sources[own_count:], front, front_sem)
    back_wait = load_chosen(config[base + 2], sources[own_count:], back, back_sem)
    step = own.shape[1] // CHUNKS
    stores = []
    for chunk in range(CHUNKS):
        rows = pl.ds(chunk * step, step)
        target = pl.ds(half * own.shape[1] + chunk * step, step)
        own_wait(chunk)

        @pl.when(has_front)
        def _():
            front_wait(chunk)

        @pl.when(has_back)
        def _():
            back_wait(chunk)

        opening = jnp.where(has_front, front[3, rows], 1.0)
        closing = jnp.where(has_back, back[3, rows], 1.0)
        passed = opening * own[3, rows]
        for channel in range(3):
            before = jnp.where(has_front, front[channel, rows], 0.0)
            behind = jnp.where(has_back, back[channel, rows], 0.0)
            made[channel, rows] = before + opening * own[channel, rows] + passed * behind
        made[3, rows] = 1.0 - passed * closing
        stores.append(pltpu.make_async_copy(made.at[:, rows, :], image.at[:, target, :], made_sem.at[chunk]))
        stores[-1].start()
    for store in stores:
        store.wait()


def finish(base, half, config, owns, gots, image):
    part = owns[0].shape
    cells = part[0] * part[1] * part[2]
    started = [] if image is None else [image]
    return pl.pallas_call(
        functools.partial(finish_kernel, base, half, len(owns)),
        out_shape=jax.ShapeDtypeStruct((part[0], HALVES * part[1], part[2]), jnp.float32),
        in_specs=[SMEM] + [ANY] * (len(owns) + len(gots) + len(started)),
        out_specs=ANY,
        scratch_shapes=[pltpu.VMEM(part, jnp.float32)] * 4 + [pltpu.SemaphoreType.DMA((CHUNKS,))] * 4,
        input_output_aliases={1 + len(owns) + len(gots): 0} if started else {},
        compiler_params=pltpu.CompilerParams(vmem_limit_bytes=50 << 20),
        cost_estimate=pl.CostEstimate(flops=4 * cells, bytes_accessed=16 * cells, transcendentals=0),
        name="finish",
    )(config, *owns, *gots, *started)


def plan(count):
    last = count - 1

    def rank(device, piece):
        return piece if device >= count // 2 else last - piece

    def source(device, ahead):
        if device == (1 if ahead else last - 1):
            return "in"
        return "odd" if (device % 2 == 0) == ahead else "even"

    ops = []
    for step in range(1, last):
        for kind in ("odd", "even"):
            senders = []
            for device in range(1, last):
                upward = (device % 2 == 1) == (kind == "odd")
                if (device <= step) if upward else (device >= last - step):
                    piece = last - step + device if upward else step + device - last
                    senders.append((device, upward, rank(device, piece), source(device, upward)))
            if senders:
                ops.append((step, kind, senders))
    rows = [[] for _ in range(count)]
    composes = {}
    for step, kind, senders in ops:
        owns = sorted({sender[2] for sender in senders})
        gots = sorted({sender[3] for sender in senders})
        composes[step, kind] = (len(rows[0]), owns, gots, [(d, d + 1 if upward else d - 1) for d, upward, _, _ in senders])
        found = {sender[0]: sender for sender in senders}
        for device in range(count):
            if device in found:
                _, upward, own, got = found[device]
                rows[device] += [1, owns.index(own), gots.index(got), int(upward)]
            else:
                rows[device] += [0, 0, 0, 0]
    owns = sorted({rank(device, device) for device in range(count)})
    gots = sorted({source(d, True) for d in range(1, count)} | {source(d, False) for d in range(last)})
    final = (len(rows[0]), owns, gots)
    for device in range(count):
        front = gots.index(source(device, True)) if device > 0 else -1
        back = gots.index(source(device, False)) if device < last else -1
        rows[device] += [owns.index(rank(device, device)), front, back]
    return composes, final, rows


def shards(density, occupancy, transfer):
    depth_cells, row_cells, col_cells = density.shape
    flags = occupancy.reshape(-1)
    block_count = flags.shape[0]
    width = col_cells // block_count
    count = lax.axis_size("depth")
    slabs = lax.axis_size("rows")
    position = lax.axis_index("depth")
    ray_step = 2.0 / (depth_cells * count)
    backward = position >= count // 2
    even = lax.rem(position, 2) == 0
    ending = jnp.logical_or(position == 0, position == count - 1)
    place = jnp.stack([backward.astype(jnp.int32), even.astype(jnp.int32), ending.astype(jnp.int32)])

    def pairs(start):
        found = []
        for low in range(start, count - 1, 2):
            found += [(low, low + 1), (low + 1, low)]
        return found

    outer, inner = pack_planes(density, flags, even.astype(jnp.int32).reshape(1), width)
    outer_plane = lax.ppermute(outer, "depth", pairs(0))
    inner_plane = lax.ppermute(inner, "depth", pairs(1)) if count > 2 else jnp.zeros_like(inner)
    first_row, last_row = pack_rows(density, flags, width)
    above = lax.ppermute(last_row, "rows", [(i, i + 1) for i in range(slabs - 1)])
    below = lax.ppermute(first_row, "rows", [(i + 1, i) for i in range(slabs - 1)])
    args = (flags, place, transfer, density, above, below)
    composes, final, rows = plan(count)
    config = lax.dynamic_index_in_dim(jnp.array(rows, jnp.int32), position, 0, keepdims=False)
    *core, _ = shade("core", 0, 1, count, ray_step, *args)
    *first, _ = shade("edge", 0, 1, count, ray_step, *args, outer_plane, *core)
    inward = [(0, 1), (count - 1, count - 2)]
    got = {("in", 0): [lax.ppermute(part, "depth", inward) for part in first]}
    pieces = {}

    def march(rank, *after):
        *pieces[rank], token = shade("full", rank, 1, count, ray_step, *args, outer_plane, inner_plane, *after)
        if rank < count - 1:
            got["in", rank] = [lax.ppermute(part, "depth", inward) for part in pieces[rank]]
        return token

    token = march(1)
    *pieces[0], token = shade("rim", 0, 1, count, ray_step, *args, outer_plane, inner_plane, *core, token)
    for step in range(1, count - 1):
        kinds = [kind for kind in ("odd", "even") if (step, kind) in composes]
        for kind in kinds:
            for rank in composes[step, kind][1]:
                if rank not in pieces:
                    token = march(rank, token)
            got[kind, step] = []
        for half in range(HALVES):
            for kind in kinds:
                base, owns, gots, pairs_of = composes[step, kind]
                part, token = compose(
                    base, config, [pieces[rank][half] for rank in owns], [got[kind_of, step - 1][half] for kind_of in gots], token
                )
                got[kind, step].append(lax.ppermute(part, "depth", pairs_of))
            if step + 1 not in pieces:
                token = march(step + 1, token)
    image = None
    base, owns, gots = final
    for half in range(HALVES):
        image = finish(
            base, half, config, [pieces[rank][half] for rank in owns], [got[kind, count - 2][half] for kind in gots], image
        )
    return image


def solution(mesh):
    in_specs = (P("depth", "rows", None), P("depth", "rows", None), P())
    out_specs = P(None, "rows", "depth")
    return jax.shard_map(shards, mesh=mesh, in_specs=in_specs, out_specs=out_specs, check_vma=False)
```

```python
import functools
import jax
import jax.numpy as jnp
from jax import lax
from jax.experimental import pallas as pl
from jax.experimental.pallas import tpu as pltpu
from jax.sharding import PartitionSpec as P

OCCUPIED_MOST = 12
PAD = 8
ROWS_AT_ONCE = 32
HALVES = 2
CHUNKS = 4
LOG2_E = 1.4426950408889634
SMEM = pl.BlockSpec(memory_space=pltpu.SMEM)
VMEM = pl.BlockSpec(memory_space=pltpu.VMEM)
ANY = pl.BlockSpec(memory_space=pl.ANY)


def pack_planes_kernel(width, flags, even, density, outer, inner, sem):
    depth_cells, row_cells, _ = density.shape
    block_count = flags.shape[0]
    slots = min(OCCUPIED_MOST, block_count)
    outer_plane = jnp.where(even[0] > 0, depth_cells - 1, 0)
    inner_plane = depth_cells - 1 - outer_plane

    def copies(block, slot):
        columns = pl.ds(pl.multiple_of(block * width, width), width)
        rows = pl.ds(pl.multiple_of(slot * row_cells, row_cells), row_cells)
        return (
            pltpu.make_async_copy(density.at[outer_plane, :, columns], outer.at[rows, :], sem.at[0, slot]),
            pltpu.make_async_copy(density.at[inner_plane, :, columns], inner.at[rows, :], sem.at[1, slot]),
        )

    def begin(block, slot):
        wanted = jnp.logical_and(flags[block] > 0, slot < slots)

        @pl.when(wanted)
        def _():
            for copy in copies(block, slot):
                copy.start()

        return slot + wanted.astype(jnp.int32)

    used = lax.fori_loop(0, block_count, begin, jnp.int32(0))
    lane = lax.broadcasted_iota(jnp.int32, (8, width), 1)
    row_of_flags = jnp.zeros((8, width), jnp.float32)
    for block in range(block_count):
        row_of_flags = jnp.where(lane == block, flags[block].astype(jnp.float32), row_of_flags)
    outer[pl.ds(slots * row_cells, 8), :] = row_of_flags
    inner[pl.ds(slots * row_cells, 8), :] = row_of_flags

    def end(slot, carry):
        for copy in copies(0, slot):
            copy.wait()
        return carry

    lax.fori_loop(0, used, end, 0)


def pack_planes(density, flags, even, width):
    row_cells = density.shape[1]
    slots = min(OCCUPIED_MOST, flags.shape[0])
    plane = jax.ShapeDtypeStruct((slots * row_cells + 8, width), jnp.float32)
    return pl.pallas_call(
        functools.partial(pack_planes_kernel, width),
        out_shape=(plane, plane),
        in_specs=[SMEM, SMEM, ANY],
        out_specs=[VMEM] * 2,
        scratch_shapes=[pltpu.SemaphoreType.DMA((2, slots))],
        compiler_params=pltpu.CompilerParams(vmem_limit_bytes=50 << 20),
        name="pack_planes",
    )(flags, even, density)


def pack_rows_kernel(width, flags, density, first_row, last_row, top, bottom, sem):
    depth_cells, row_cells, _ = density.shape
    block_count = flags.shape[0]
    top_copy = pltpu.make_async_copy(density.at[:, 0:8, :], top, sem.at[0])
    bottom_copy = pltpu.make_async_copy(density.at[:, row_cells - 8 : row_cells, :], bottom, sem.at[1])
    top_copy.start()
    bottom_copy.start()
    top_copy.wait()
    bottom_copy.wait()

    def edge(block, carry):
        columns = pl.ds(pl.multiple_of(block * width, width), width)
        flag = flags[block].astype(jnp.float32)
        for z in range(depth_cells):
            first_row[pl.ds(z, 1), columns] = top[z, 0:1, columns] * flag
            last_row[pl.ds(z, 1), columns] = bottom[z, 7:8, columns] * flag
        return carry

    lax.fori_loop(0, block_count, edge, 0)


def pack_rows(density, flags, width):
    depth_cells, _, col_cells = density.shape
    row = jax.ShapeDtypeStruct((depth_cells, col_cells), jnp.float32)
    return pl.pallas_call(
        functools.partial(pack_rows_kernel, width),
        out_shape=(row, row),
        in_specs=[SMEM, ANY],
        out_specs=[VMEM] * 2,
        scratch_shapes=[
            pltpu.VMEM((depth_cells, 8, col_cells), jnp.float32),
            pltpu.VMEM((depth_cells, 8, col_cells), jnp.float32),
            pltpu.SemaphoreType.DMA((2,)),
        ],
        compiler_params=pltpu.CompilerParams(vmem_limit_bytes=50 << 20),
        name="pack_rows",
    )(flags, density)


def shade_kernel(mode, first_at, piece_count, piece_total, width, ray_step, flags, place, transfer, density, above, below, *others):
    plane_count = {"core": 0, "edge": 1, "rim": 2, "full": 2}[mode]
    thin = mode in ("edge", "rim")
    planes = others[:plane_count]
    others = others[plane_count:]
    if thin:
        core, others = others[:HALVES], others[HALVES:]
    *others, token, vol, side_flags, block_sem, plane_sem, flag_sem, stage, stage_sem = others
    outs = targets = others[-HALVES * piece_count :]
    if thin:
        outs = [stage.at[half] for half in range(HALVES)]
    token[0] = flags[0]
    depth_cells, row_cells, _ = density.shape
    block_count = flags.shape[0]
    piece_blocks = block_count // piece_total
    slots = min(OCCUPIED_MOST, block_count)
    backward = place[0] > 0
    even = place[1] > 0
    ending = place[2] > 0
    own = piece_count * piece_blocks
    zero_slot = own + 2
    first_piece = jnp.where(backward, first_at, piece_total - first_at - piece_count)
    first_block = first_piece * piece_blocks
    body = pl.ds(PAD, row_cells)
    half_rows = row_cells // HALVES
    if thin:
        held = [(1, 0, 2), (3, depth_cells - 2, 2)]
        runs = [[(1, 0)], [(4, depth_cells - 1)]]
        low_at, high_at = 0, 5
    else:
        held = [(1, 0, depth_cells)]
        trim = 1 if mode == "core" else 0
        runs = [[(z + 1, z) for z in range(trim, depth_cells - trim)]]
        low_at, high_at = 0, depth_cells + 1

    def put(piece_at, half, rows, columns, values):
        for at in range(piece_count):
            for part in range(HALVES):

                @pl.when(jnp.logical_and(piece_at == at, half == part))
                def _():
                    for channel in range(4):
                        outs[at * HALVES + part][channel, rows, columns] = values[channel]

    def block_of(slot):
        return first_block + slot - 1

    def occupied(block):
        inside = jnp.logical_and(block >= 0, block < block_count)
        return jnp.logical_and(inside, flags[jnp.clip(block, 0, block_count - 1)] > 0)

    def block_copies(slot):
        block = jnp.clip(block_of(slot), 0, block_count - 1)
        columns = pl.ds(pl.multiple_of(block * width, width), width)
        return [
            pltpu.make_async_copy(
                density.at[pl.ds(z, count), :, columns], vol.at[slot, pl.ds(at, count), body, :], block_sem.at[part, slot]
            )
            for part, (at, z, count) in enumerate(held)
        ]

    def plane_copy(side, which, slot, rank):
        rows = pl.ds(pl.multiple_of(rank * row_cells, row_cells), row_cells)
        at = high_at if side else low_at
        return pltpu.make_async_copy(planes[which].at[rows, :], vol.at[slot, at, body, :], plane_sem.at[side, slot])

    def near(side, block):
        if mode == "edge":
            return jnp.logical_and(backward if side == 0 else jnp.logical_not(backward), side_flags[0, 0, block] > 0.5)
        which = jnp.where(even, 1 - side, side)
        return side_flags[which, 0, block] > 0.5

    def begin_block(slot, carry):
        @pl.when(occupied(block_of(slot)))
        def _():
            for copy in block_copies(slot):
                copy.start()

        return carry

    def begin_plane(block, ranks):
        slot = block - first_block + 1
        mine = jnp.logical_and(jnp.logical_and(slot >= 1, slot <= own), flags[block] > 0)
        after_this = []
        for side in range(2):
            close = near(side, block)
            wanted = jnp.logical_and(mine, close)
            for which in range(2):
                chosen = even if which != side else jnp.logical_not(even)

                @pl.when(jnp.logical_and(wanted, chosen))
                def _():
                    plane_copy(side, which, slot, ranks[side]).start()

            after_this.append(ranks[side] + close.astype(jnp.int32))
        return tuple(after_this)

    def arrive(slot):
        @pl.when(occupied(block_of(slot)))
        def _():
            for copy in block_copies(slot):
                copy.wait()

    def later_ranks(block, ranks):
        return tuple(rank + jnp.where(side_flags[which, 0, block] > 0.5, 1, 0) for which, rank in enumerate(ranks))

    def visit(slot, carry):
        block = block_of(slot)
        piece = block // piece_blocks - first_piece
        at = jnp.where(backward, piece, piece_count - 1 - piece)
        columns = pl.ds(pl.multiple_of(lax.rem(block, piece_blocks) * width, width), width)
        arrive(slot + 1)

        @pl.when(jnp.logical_not(occupied(block)))
        def _():
            blank = jnp.zeros((half_rows, width), jnp.float32)
            for half in range(HALVES):
                put(at, half, slice(None), columns, [blank, blank, blank, blank + 1.0])

        @pl.when(occupied(block))
        def _():
            left = jnp.where(occupied(block - 1), slot - 1, zero_slot)
            right = jnp.where(occupied(block + 1), slot + 1, zero_slot)
            source = pl.ds(pl.multiple_of(block * width, width), width)
            for run in runs:
                for z, depth in run:
                    vol[slot, z, pl.ds(PAD - 1, 1), :] = above[pl.ds(depth, 1), source]
                    vol[slot, z, pl.ds(PAD + row_cells, 1), :] = below[pl.ds(depth, 1), source]
            for side in range(2 if planes else 0):
                close = near(side, block)
                side_at = high_at if side else low_at

                if mode == "full":

                    @pl.when(close)
                    def _():
                        plane_copy(side, 0, slot, 0).wait()

                else:
                    for which in range(plane_count):
                        chosen = True if plane_count == 1 else (even if which != side else jnp.logical_not(even))

                        @pl.when(jnp.logical_and(close, chosen))
                        def _():
                            rows = pl.ds(pl.multiple_of(carry[which] * row_cells, row_cells), row_cells)
                            vol[slot, side_at, body, :] = planes[which][rows, :]

                @pl.when(jnp.logical_not(close))
                def _():
                    vol[slot, side_at, body, :] = jnp.zeros((row_cells, width), jnp.float32)

            march(slot, left, right, at, columns)

        return carry if not thin else later_ranks(block, carry)

    def march(slot, left, right, piece_at, columns):
        rows_at_once = half_rows if thin else min(ROWS_AT_ONCE, half_rows)
        shape = (rows_at_once, width)
        lane = lax.broadcasted_iota(jnp.int32, shape, 1)
        at_first = lane == 0
        at_last = lane == width - 1
        slopes = [transfer[0, channel] * 0.5 for channel in range(3)]
        offsets = [transfer[1, channel] * 0.5 for channel in range(3)]
        decay_slope = transfer[0, 3] * LOG2_E
        decay_offset = transfer[1, 3] * LOG2_E

        def shaded(run, start):
            rows = pl.ds(start, rows_at_once)
            previous = vol[slot, run[0][0] - 1, rows, :]
            center = vol[slot, run[0][0], rows, :]
            transmit = jnp.ones(shape, jnp.float32)
            plain = jnp.zeros(shape, jnp.float32)
            tinted = [plain] * 3
            for z, _ in run:
                following = vol[slot, z + 1, rows, :]
                diff_z = following - previous
                diff_y = vol[slot, z, pl.ds(start + 1, rows_at_once), :] - vol[slot, z, pl.ds(start - 1, rows_at_once), :]
                right_side = pltpu.roll(jnp.where(at_first, vol[right, z, rows, :], center), width - 1, 1)
                left_side = pltpu.roll(jnp.where(at_last, vol[left, z, rows, :], center), 1, 1)
                diff_x = right_side - left_side
                facing = jnp.abs(diff_x + 0.9375 * diff_y + 0.75 * diff_z)
                norm = lax.rsqrt(diff_x * diff_x + diff_y * diff_y + (diff_z * diff_z + 4.0))
                lighting = facing * norm + (0.3 / 0.448)
                soft = lax.log2(1.0 + jnp.exp2(decay_slope * center + decay_offset))
                passed = transmit * jnp.exp2((center * -ray_step) * soft)
                weight = (transmit - passed) * lighting
                transmit = passed
                plain = plain + weight
                tinted = [
                    tinted[channel] + weight * jnp.tanh(slopes[channel] * center + offsets[channel]) for channel in range(3)
                ]
                previous, center = center, following
            return [0.224 * (plain + tinted[channel]) for channel in range(3)], transmit

        def chunk(half, at):
            start = pl.multiple_of(PAD + half * half_rows + at * rows_at_once, 8)
            target = pl.ds(pl.multiple_of(at * rows_at_once, 8), rows_at_once)
            colors, transmit = shaded(runs[0], start)
            if thin:
                inner = core[half][3, target, columns]
                back_colors, back_transmit = shaded(runs[1], start)
                colors = [
                    colors[channel] + transmit * (core[half][channel, target, columns] + inner * back_colors[channel])
                    for channel in range(3)
                ]
                transmit = transmit * inner * back_transmit
            put(piece_at, half, target, columns, colors + [transmit])

        per_half = half_rows // rows_at_once
        if thin:
            for half in range(HALVES):
                chunk(half, 0)
        else:
            lax.fori_loop(0, HALVES * per_half, lambda at, carry: chunk(at // per_half, lax.rem(at, per_half)) or carry, 0)

    def work():
        flag_rows = pl.ds(slots * row_cells, 8)
        flag_copies = [
            pltpu.make_async_copy(plane.at[flag_rows, :], side_flags.at[which], flag_sem.at[which])
            for which, plane in enumerate(planes)
        ]
        for copy in flag_copies:
            copy.start()
        lax.fori_loop(0, own + 2, begin_block, 0)
        for run in runs:
            for z, _ in run:
                vol[zero_slot, z, body, :] = jnp.zeros((row_cells, width), jnp.float32)
        for copy in flag_copies:
            copy.wait()
        if mode == "full":
            lax.fori_loop(0, block_count, begin_plane, (jnp.int32(0), jnp.int32(0)))
        arrive(0)
        arrive(1)
        ranks = lax.fori_loop(0, first_block, later_ranks, (jnp.int32(0),) * plane_count) if thin else 0
        lax.fori_loop(1, own + 1, visit, ranks)
        if thin:
            stores = [pltpu.make_async_copy(out, target, stage_sem.at[at]) for at, (out, target) in enumerate(zip(outs, targets))]
            for store in stores:
                store.start()
            for store in stores:
                store.wait()

    if thin:
        pl.when(ending if mode == "edge" else jnp.logical_not(ending))(work)
    else:
        work()


def shade(mode, first_at, piece_count, piece_total, ray_step, flags, place, transfer, density, above, below, *others):
    depth_cells, row_cells, col_cells = density.shape
    block_count = flags.shape[0]
    width = col_cells // block_count
    own = piece_count * (block_count // piece_total)
    thin = mode in ("edge", "rim")
    depth = 2 if thin else depth_cells
    cells = own * depth * row_cells * width
    held = 6 if thin else depth_cells + 2
    part = (4, row_cells // HALVES, col_cells // piece_total)
    out = jax.ShapeDtypeStruct(part, jnp.float32)
    outs = HALVES * piece_count
    extra = {"core": [], "edge": [VMEM] * (1 + HALVES), "rim": [VMEM] * (2 + HALVES), "full": [ANY] * 2}[mode]
    extra = extra + [SMEM] * (len(others) - len(extra))
    return pl.pallas_call(
        functools.partial(shade_kernel, mode, first_at, piece_count, piece_total, width, ray_step),
        out_shape=(out,) * outs + (jax.ShapeDtypeStruct((1,), jnp.int32),),
        in_specs=[SMEM] * 3 + [ANY] + [VMEM] * 2 + extra,
        out_specs=(ANY if thin else VMEM,) * outs + (SMEM,),
        scratch_shapes=[
            pltpu.VMEM((own + 3, held, row_cells + 2 * PAD, width), jnp.float32),
            pltpu.SMEM((2, 8, width), jnp.float32),
            pltpu.SemaphoreType.DMA((2, own + 2)),
            pltpu.SemaphoreType.DMA((2, own + 2)),
            pltpu.SemaphoreType.DMA((2,)),
            pltpu.VMEM((HALVES,) + part if thin else (1, 8, 128), jnp.float32),
            pltpu.SemaphoreType.DMA((HALVES,)),
        ],
        compiler_params=pltpu.CompilerParams(vmem_limit_bytes=50 << 20),
        cost_estimate=pl.CostEstimate(flops=60 * cells, bytes_accessed=4 * cells, transcendentals=7 * cells),
    )(flags, place, transfer, density, above, below, *others)


def load_chosen(chosen, sources, buffer, sem):
    step = buffer.shape[1] // CHUNKS
    for at, source in enumerate(sources):

        @pl.when(chosen == at)
        def _():
            for chunk in range(CHUNKS):
                rows = pl.ds(chunk * step, step)
                pltpu.make_async_copy(source.at[:, rows, :], buffer.at[:, rows, :], sem.at[chunk]).start()

    def wait(chunk):
        rows = pl.ds(chunk * step, step)
        pltpu.make_async_copy(sources[0].at[:, rows, :], buffer.at[:, rows, :], sem.at[chunk]).wait()

    return wait


def compose_kernel(base, own_count, config, *others):
    *sources, _, out, token, own, got, made, own_sem, got_sem, made_sem = others
    step = own.shape[1] // CHUNKS
    token[0] = config[0]

    @pl.when(config[base] > 0)
    def _():
        own_wait = load_chosen(config[base + 1], sources[:own_count], own, own_sem)
        got_wait = load_chosen(config[base + 2], sources[own_count:], got, got_sem)
        stores = []
        for chunk in range(CHUNKS):
            rows = pl.ds(chunk * step, step)
            own_wait(chunk)
            got_wait(chunk)
            for upward, front, back in ((True, got, own), (False, own, got)):

                @pl.when((config[base + 3] > 0) == upward)
                def _():
                    passed = front[3, rows]
                    for channel in range(3):
                        made[channel, rows] = front[channel, rows] + passed * back[channel, rows]
                    made[3, rows] = passed * back[3, rows]

            stores.append(pltpu.make_async_copy(made.at[:, rows, :], out.at[:, rows, :], made_sem.at[chunk]))
            stores[-1].start()
        for store in stores:
            store.wait()


def compose(base, config, owns, gots, after):
    part = owns[0].shape
    cells = part[0] * part[1] * part[2]
    return pl.pallas_call(
        functools.partial(compose_kernel, base, len(owns)),
        out_shape=(jax.ShapeDtypeStruct(part, jnp.float32), jax.ShapeDtypeStruct((1,), jnp.int32)),
        in_specs=[SMEM] + [ANY] * (len(owns) + len(gots)) + [SMEM],
        out_specs=(ANY, SMEM),
        scratch_shapes=[pltpu.VMEM(part, jnp.float32)] * 3 + [pltpu.SemaphoreType.DMA((CHUNKS,))] * 3,
        compiler_params=pltpu.CompilerParams(vmem_limit_bytes=50 << 20),
        cost_estimate=pl.CostEstimate(flops=2 * cells, bytes_accessed=12 * cells, transcendentals=0),
        name="compose",
    )(config, *owns, *gots, after)


def finish_kernel(base, half, own_count, config, *others):
    *sources, image, own, front, back, made, own_sem, front_sem, back_sem, made_sem = others
    if half:
        sources = sources[:-1]
    has_front, has_back = config[base + 1] >= 0, config[base + 2] >= 0
    own_wait = load_chosen(config[base], sources[:own_count], own, own_sem)
    front_wait = load_chosen(config[base + 1], sources[own_count:], front, front_sem)
    back_wait = load_chosen(config[base + 2], sources[own_count:], back, back_sem)
    step = own.shape[1] // CHUNKS
    stores = []
    for chunk in range(CHUNKS):
        rows = pl.ds(chunk * step, step)
        target = pl.ds(half * own.shape[1] + chunk * step, step)
        own_wait(chunk)

        @pl.when(has_front)
        def _():
            front_wait(chunk)

        @pl.when(has_back)
        def _():
            back_wait(chunk)

        opening = jnp.where(has_front, front[3, rows], 1.0)
        closing = jnp.where(has_back, back[3, rows], 1.0)
        passed = opening * own[3, rows]
        for channel in range(3):
            before = jnp.where(has_front, front[channel, rows], 0.0)
            behind = jnp.where(has_back, back[channel, rows], 0.0)
            made[channel, rows] = before + opening * own[channel, rows] + passed * behind
        made[3, rows] = 1.0 - passed * closing
        stores.append(pltpu.make_async_copy(made.at[:, rows, :], image.at[:, target, :], made_sem.at[chunk]))
        stores[-1].start()
    for store in stores:
        store.wait()


def finish(base, half, config, owns, gots, image):
    part = owns[0].shape
    cells = part[0] * part[1] * part[2]
    started = [] if image is None else [image]
    return pl.pallas_call(
        functools.partial(finish_kernel, base, half, len(owns)),
        out_shape=jax.ShapeDtypeStruct((part[0], HALVES * part[1], part[2]), jnp.float32),
        in_specs=[SMEM] + [ANY] * (len(owns) + len(gots) + len(started)),
        out_specs=ANY,
        scratch_shapes=[pltpu.VMEM(part, jnp.float32)] * 4 + [pltpu.SemaphoreType.DMA((CHUNKS,))] * 4,
        input_output_aliases={1 + len(owns) + len(gots): 0} if started else {},
        compiler_params=pltpu.CompilerParams(vmem_limit_bytes=50 << 20),
        cost_estimate=pl.CostEstimate(flops=4 * cells, bytes_accessed=16 * cells, transcendentals=0),
        name="finish",
    )(config, *owns, *gots, *started)


def plan(count):
    last = count - 1

    def rank(device, piece):
        return piece if device >= count // 2 else last - piece

    def source(device, ahead):
        if device == (1 if ahead else last - 1):
            return "in"
        return "odd" if (device % 2 == 0) == ahead else "even"

    ops = []
    for step in range(1, last):
        for kind in ("odd", "even"):
            senders = []
            for device in range(1, last):
                upward = (device % 2 == 1) == (kind == "odd")
                if (device <= step) if upward else (device >= last - step):
                    piece = last - step + device if upward else step + device - last
                    senders.append((device, upward, rank(device, piece), source(device, upward)))
            if senders:
                ops.append((step, kind, senders))
    rows = [[] for _ in range(count)]
    composes = {}
    for step, kind, senders in ops:
        owns = sorted({sender[2] for sender in senders})
        gots = sorted({sender[3] for sender in senders})
        composes[step, kind] = (len(rows[0]), owns, gots, [(d, d + 1 if upward else d - 1) for d, upward, _, _ in senders])
        found = {sender[0]: sender for sender in senders}
        for device in range(count):
            if device in found:
                _, upward, own, got = found[device]
                rows[device] += [1, owns.index(own), gots.index(got), int(upward)]
            else:
                rows[device] += [0, 0, 0, 0]
    owns = sorted({rank(device, device) for device in range(count)})
    gots = sorted({source(d, True) for d in range(1, count)} | {source(d, False) for d in range(last)})
    final = (len(rows[0]), owns, gots)
    for device in range(count):
        front = gots.index(source(device, True)) if device > 0 else -1
        back = gots.index(source(device, False)) if device < last else -1
        rows[device] += [owns.index(rank(device, device)), front, back]
    return composes, final, rows


def shards(density, occupancy, transfer):
    depth_cells, _, col_cells = density.shape
    flags = occupancy.reshape(-1)
    block_count = flags.shape[0]
    width = col_cells // block_count
    count = lax.axis_size("depth")
    slabs = lax.axis_size("rows")
    position = lax.axis_index("depth")
    ray_step = 2.0 / (depth_cells * count)
    backward = position >= count // 2
    even = lax.rem(position, 2) == 0
    ending = jnp.logical_or(position == 0, position == count - 1)
    place = jnp.stack([backward.astype(jnp.int32), even.astype(jnp.int32), ending.astype(jnp.int32)])

    def pairs(start):
        found = []
        for low in range(start, count - 1, 2):
            found += [(low, low + 1), (low + 1, low)]
        return found

    outer, inner = pack_planes(density, flags, even.astype(jnp.int32).reshape(1), width)
    outer_plane = lax.ppermute(outer, "depth", pairs(0))
    inner_plane = lax.ppermute(inner, "depth", pairs(1)) if count > 2 else jnp.zeros_like(inner)
    first_row, last_row = pack_rows(density, flags, width)
    above = lax.ppermute(last_row, "rows", [(i, i + 1) for i in range(slabs - 1)])
    below = lax.ppermute(first_row, "rows", [(i + 1, i) for i in range(slabs - 1)])
    args = (flags, place, transfer, density, above, below)
    composes, final, rows = plan(count)
    config = lax.dynamic_index_in_dim(jnp.array(rows, jnp.int32), position, 0, keepdims=False)
    *core, _ = shade("core", 0, 1, count, ray_step, *args)
    *first, _ = shade("edge", 0, 1, count, ray_step, *args, outer_plane, *core)
    inward = [(0, 1), (count - 1, count - 2)]
    got = {("in", 0): [lax.ppermute(part, "depth", inward) for part in first]}
    pieces = {}

    def send(parts, route):
        arrived = []
        for part in parts:
            arrived.append(lax.ppermute(part, "depth", route))
        return arrived

    def march(rank, *after):
        *pieces[rank], token = shade("full", rank, 1, count, ray_step, *args, outer_plane, inner_plane, *after)
        if rank < count - 1:
            got["in", rank] = send(pieces[rank], inward)
        return token

    token = march(1)
    *pieces[0], token = shade("rim", 0, 1, count, ray_step, *args, outer_plane, inner_plane, *core, token)
    for step in range(1, count - 1):
        kinds = [kind for kind in ("even", "odd") if (step, kind) in composes]
        for kind in kinds:
            for rank in composes[step, kind][1]:
                if rank not in pieces:
                    token = march(rank, token)
            got[kind, step] = []
        for half in range(HALVES):
            for kind in kinds:
                base, owns, gots, pairs_of = composes[step, kind]
                part, token = compose(
                    base, config, [pieces[rank][half] for rank in owns], [got[kind_of, step - 1][half] for kind_of in gots], token
                )
                got[kind, step].append(lax.ppermute(part, "depth", pairs_of))
            if step + 1 not in pieces:
                token = march(step + 1, token)
    image = None
    base, owns, gots = final
    for half in range(HALVES):
        image = finish(
            base, half, config, [pieces[rank][half] for rank in owns], [got[kind, count - 2][half] for kind in gots], image
        )
    return image


def solution(mesh):
    in_specs = (P("depth", "rows", None), P("depth", "rows", None), P())
    out_specs = P(None, "rows", "depth")
    return jax.shard_map(shards, mesh=mesh, in_specs=in_specs, out_specs=out_specs, check_vma=False)
```
